32 devices in a mesh: groups: 2 (over y), ctx: 4 (over z), head: 2 (over x), role: 2 (over core).
Axes of the slice: x: 2, y: 2, z: 4, core: 2. Of those that a mesh axis runs over, the one named last changes fastest.
Arguments:
- prompt_query: bfloat16 [768, 64, 192], P(('groups', 'ctx'), ('head', 'role')), parts along dimension 0, may hold values from -200 to 200
- prompt_latent: bfloat16 [768, 576], P(('groups', 'ctx')), parts along dimension 0, may hold values from -60 to 60
- block_order: int32 [8], P('groups'), parts along dimension 0, may hold values from 0 to 3, as said below
- key_up: bfloat16 [64, 128, 512], P(('head', 'role')), may hold values from -0.5 to 0.5
- value_up: bfloat16 [64, 512, 128], P(('head', 'role')), may hold values from -1.796875 to 1.796875
- out_weight: bfloat16 [8192, 7168], P(('head', 'role'), 'ctx'), may hold values from -0.0625 to 0.0625
- step_query: bfloat16 [4, 8, 64, 192], P(None, 'groups', ('head', 'role')), parts along dimension 1, may hold values from -200 to 200
- cache_latent: bfloat16 [8, 1536, 576], P('groups', 'ctx'), parts along dimension 0, may hold values from -60 to 60
- step_latent: bfloat16 [4, 8, 576], P(None, 'groups'), parts along dimension 1, may hold values from -5 to 5
- cache_length: int32 [8], P('groups'), parts along dimension 0, may hold values from 2 to 1536
- block_dest: int32 [8], P('groups'), parts along dimension 0, may hold values from 0 to 3
Outputs:
- prompt_out: bfloat16 [768, 8192], P(('groups', 'ctx'), ('head', 'role')), parts along dimension 0
- step_out: bfloat16 [4, 8, 7168], P(None, 'groups', ('ctx', 'head', 'role')), parts along dimension 1
The draws below stay inside these ranges and needn't reach their ends.
There are 2 independent parts, one for each index of `groups`. The reference program is written for one: setup_inputs(seed, part) draws one part's arguments, and reference() takes and returns one part's arrays. A program takes and returns all parts, laid end to end along the dimension named above; an argument that names none is the same for every part. Nothing has to cross between parts.
Inputs may be any that keep to these rules, and one draw needn't show every extreme that they name: `block_order`: a permutation: each block position appears once.
All inputs are finite; a program needn't handle non-finite values.
Results may differ from the reference program's by a relative error of at most 0.039.
Values may be sent and summed in bfloat16 or wider, within the bound.
No kernel may reach another device: no remote copies, remote signals or barrier semaphores. Data moves between devices by JAX's collectives and lax.ppermute only.
A program may use at most 64 MiB of HBM per device.

```python
import jax
import jax.numpy as jnp
from jax import lax

HEADS = 64
NOPE = 128
ROPE = 64
LATENT = 512
VDIM = 128
DMODEL = 7168
STEPS = 4
ROWS = 4
TOK_DEV = 96
SEQ = 384
CACHE = 1536
N_CTX = 4


def prompt_order(key):
    return jax.random.permutation(jax.random.fold_in(key, 101), N_CTX).astype(jnp.int32)


def prompt_keys(key):
    values = jnp.clip(jax.random.normal(jax.random.fold_in(key, 102), (SEQ, LATENT + ROPE), jnp.float32), -5.0, 5.0)
    return values


def cache_keys(key):
    values = jnp.clip(jax.random.normal(jax.random.fold_in(key, 202), (ROWS, CACHE, LATENT + ROPE), jnp.float32), -5.0, 5.0)
    return values


def draw_block_order(key, part):
    return prompt_order(key)


def draw_prompt_latent(key, part):
    return prompt_keys(key).astype(jnp.bfloat16)


def draw_cache_latent(key, part):
    return cache_keys(key).astype(jnp.bfloat16)


def draw_prompt_query(key, part):
    values = jnp.clip(jax.random.normal(jax.random.fold_in(key, 104), (SEQ, HEADS, NOPE + ROPE), jnp.float32), -5.0, 5.0)
    return values.astype(jnp.bfloat16)


def draw_step_query(key, part):
    values = jnp.clip(jax.random.normal(jax.random.fold_in(key, 204), (STEPS, ROWS, HEADS, NOPE + ROPE), jnp.float32), -5.0, 5.0)
    return values.astype(jnp.bfloat16)


def set_ends(drawn, key, least, largest):
    longest = drawn.shape.index(max(drawn.shape))
    spots = []
    for shift in (0, 1):
        where = [jax.random.randint(jax.random.fold_in(key, axis), (), 0, length) for axis, length in enumerate(drawn.shape)]
        where[longest] = (where[longest] + shift) % drawn.shape[longest]
        spots.append(tuple(where))
    return drawn.at[spots[0]].set(least).at[spots[1]].set(largest)


def block_scale(key, dims, pieces, smallest, high):
    gain = 1.0
    for dim, parts in pieces:
        draws = jax.random.uniform(jax.random.fold_in(jax.random.fold_in(key, 6), dim), (parts,), jnp.float32, smallest / len(pieces), high / len(pieces))
        gain = gain * jnp.repeat(jnp.exp(draws), dims[dim] // parts).reshape((-1,) + (1,) * (len(dims) - 1 - dim))
    return gain


def normal_values(rng, extent, spread, bound, shards=(), kind=jnp.bfloat16):
    gain = block_scale(rng, extent, shards, -0.22, 0.18) if shards else 1.0
    result = jax.random.normal(rng, extent, jnp.float32) * spread * gain
    return jnp.minimum(jnp.maximum(result, -bound), bound).astype(kind)


def setup_inputs(seed: int = 0, part: int = 0) -> dict:
    keys = jax.random.split(jax.random.key(seed), 12)
    part_keys = jax.random.split(jax.random.fold_in(keys[11], part), 12)
    return {
        "prompt_query": draw_prompt_query(jax.random.fold_in(jax.random.fold_in(keys[11], part), 71), part),
        "prompt_latent": draw_prompt_latent(jax.random.fold_in(jax.random.fold_in(keys[11], part), 71), part),
        "block_order": draw_block_order(jax.random.fold_in(jax.random.fold_in(keys[11], part), 71), part),
        "key_up": normal_values(keys[3], (HEADS, NOPE, LATENT), NOPE ** -0.5, 0.5, ((0, 4),)),
        "value_up": normal_values(keys[4], (HEADS, LATENT, VDIM), 0.3, 1.796875, ((0, 4),)),
        "out_weight": normal_values(keys[5], (HEADS * VDIM, DMODEL), (HEADS * VDIM) ** -0.5, 0.0625, ((0, 4), (1, 4))),
        "step_query": draw_step_query(jax.random.fold_in(jax.random.fold_in(keys[11], part), 71), part),
        "cache_latent": draw_cache_latent(jax.random.fold_in(jax.random.fold_in(keys[11], part), 71), part),
        "step_latent": normal_values(part_keys[8], (STEPS, ROWS, LATENT + ROPE), 1.0, 5.0),
        "cache_length": set_ends(jax.random.randint(part_keys[9], (ROWS,), 2, CACHE + 1), jax.random.fold_in(part_keys[9], 1), 2, CACHE).astype(jnp.int32),
        "block_dest": set_ends(jax.random.randint(part_keys[10], (N_CTX,), 0, ROWS), jax.random.fold_in(part_keys[10], 1), 0, ROWS - 1).astype(jnp.int32),
    }


def absorbed(queries, key_up):
    latent_part = jnp.einsum('...hn,hnc->...hc', queries[..., :NOPE].astype(jnp.float32), key_up.astype(jnp.float32)).astype(jnp.bfloat16)
    return jnp.concatenate([latent_part, queries[..., NOPE:]], axis=-1)


def reference(prompt_query, prompt_latent, block_order, key_up, value_up, out_weight, step_query, cache_latent, step_latent, cache_length, block_dest):
    score_scale = (NOPE + ROPE) ** -0.5
    position = (block_order[:, None] * TOK_DEV + jnp.arange(TOK_DEV, dtype=jnp.int32)[None, :]).reshape(SEQ).astype(jnp.int32)
    prompt_rows = absorbed(prompt_query, key_up)
    visible = position[None, :] <= position[:, None]

    def one_head(inputs):
        head_rows, head_value = inputs
        scores = jnp.dot(head_rows, prompt_latent.T, preferred_element_type=jnp.float32) * score_scale
        scores = jnp.where(visible, scores, jnp.float32(-1e30))
        highest = jnp.max(scores, axis=1)
        weights = jnp.where(visible, jnp.exp(scores - highest[:, None]), jnp.float32(0.0))
        totals = jnp.sum(weights, axis=1)
        summed = jnp.dot(weights.astype(jnp.bfloat16), prompt_latent[:, :LATENT], preferred_element_type=jnp.float32)
        attended = (summed / totals[:, None]).astype(jnp.bfloat16)
        return jnp.dot(attended, head_value, preferred_element_type=jnp.float32).astype(jnp.bfloat16)

    head_outs = lax.map(one_head, (jnp.transpose(prompt_rows, (1, 0, 2)), value_up))
    prompt_out = jnp.transpose(head_outs, (1, 0, 2)).reshape(SEQ, HEADS * VDIM)

    step_rows = absorbed(step_query, key_up).astype(jnp.float32)
    cache_scores = jnp.einsum('sbhc,bpc->sbhp', step_rows, cache_latent.astype(jnp.float32)) * score_scale
    live_mask = (jnp.arange(CACHE, dtype=jnp.int32)[None, :] < cache_length[:, None])[None, :, None, :]
    cache_scores = jnp.where(live_mask, cache_scores, jnp.float32(-1e30))
    token_block = (jnp.arange(SEQ, dtype=jnp.int32) // TOK_DEV).astype(jnp.int32)
    handed = (block_dest[token_block][None, :] == jnp.arange(ROWS, dtype=jnp.int32)[:, None])[None, :, None, :]
    handed_scores = jnp.einsum('sbhc,jc->sbhj', step_rows, prompt_latent.astype(jnp.float32)) * score_scale
    handed_scores = jnp.where(handed, handed_scores, jnp.float32(-1e30))
    fresh_scores = jnp.einsum('sbhc,ubc->sbhu', step_rows, step_latent.astype(jnp.float32)) * score_scale
    step_ids = jnp.arange(STEPS, dtype=jnp.int32)
    order_mask = (step_ids[None, :] <= step_ids[:, None])[:, None, None, :]
    fresh_scores = jnp.where(order_mask, fresh_scores, jnp.float32(-1e30))
    highest = jnp.maximum(jnp.maximum(jnp.max(cache_scores, axis=-1), jnp.max(fresh_scores, axis=-1)), jnp.max(handed_scores, axis=-1))
    cache_weights = jnp.where(live_mask, jnp.exp(cache_scores - highest[..., None]), jnp.float32(0.0))
    handed_weights = jnp.where(handed, jnp.exp(handed_scores - highest[..., None]), jnp.float32(0.0))
    fresh_weights = jnp.where(order_mask, jnp.exp(fresh_scores - highest[..., None]), jnp.float32(0.0))
    totals = jnp.sum(cache_weights, axis=-1) + jnp.sum(handed_weights, axis=-1) + jnp.sum(fresh_weights, axis=-1)
    summed = jnp.einsum('sbhp,bpc->sbhc', cache_weights.astype(jnp.bfloat16).astype(jnp.float32), cache_latent[..., :LATENT].astype(jnp.float32))
    summed = summed + jnp.einsum('sbhj,jc->sbhc', handed_weights.astype(jnp.bfloat16).astype(jnp.float32), prompt_latent[:, :LATENT].astype(jnp.float32))
    summed = summed + jnp.einsum('sbhu,ubc->sbhc', fresh_weights.astype(jnp.bfloat16).astype(jnp.float32), step_latent[..., :LATENT].astype(jnp.float32))
    attended = (summed / totals[..., None]).astype(jnp.bfloat16)
    step_heads = jnp.einsum('sbhc,hcv->sbhv', attended.astype(jnp.float32), value_up.astype(jnp.float32)).astype(jnp.bfloat16)
    step_heads = step_heads.reshape(STEPS * ROWS, HEADS * VDIM)
    step_out = jnp.dot(step_heads, out_weight, preferred_element_type=jnp.float32).astype(jnp.bfloat16).reshape(STEPS, ROWS, DMODEL)
    return prompt_out, step_out
```

```python
import jax
import jax.numpy as jnp
from jax import lax
from jax.sharding import PartitionSpec as P


def absorbed(queries, key_up):
    nope_width = key_up.shape[1]
    latent_part = jnp.einsum(
        "...hn,hnc->...hc", queries[..., :nope_width], key_up, preferred_element_type=jnp.float32
    ).astype(jnp.bfloat16)
    return jnp.concatenate([latent_part, queries[..., nope_width:]], axis=-1)


def swap(value, axis, step):
    size = lax.axis_size(axis)
    return lax.ppermute(value, axis, [(i, i ^ step) for i in range(size)])


def doublings(size):
    steps = []
    step = 1
    while step < size:
        steps.append(step)
        step *= 2
    assert step == size
    return steps


def combine(first_part, second_part):
    high_a, totals_a, mixed_a = first_part
    high_b, totals_b, mixed_b = second_part
    highest = jnp.maximum(high_a, high_b)
    share_a = totals_a * jnp.exp(high_a - highest)
    share_b = totals_b * jnp.exp(high_b - highest)
    totals = share_a + share_b
    safe = jnp.maximum(totals, 1e-30)
    mixed = (
        mixed_a.astype(jnp.float32) * (share_a / safe)[..., None]
        + mixed_b.astype(jnp.float32) * (share_b / safe)[..., None]
    )
    return highest, totals, mixed


def per_device(
    prompt_query,
    prompt_latent,
    block_order,
    key_up,
    value_up,
    out_weight,
    step_query,
    cache_latent,
    step_latent,
    cache_length,
    block_dest,
):
    tokens, head_count, query_width = prompt_query.shape
    latent_width = key_up.shape[2]
    score_scale = query_width ** (-0.5)
    context_size = lax.axis_size("ctx")
    place = lax.axis_index("ctx")
    slot_ids = jnp.arange(context_size)
    step_count, row_count = (step_query.shape[0], step_query.shape[1])
    cache_span = cache_latent.shape[1]

    role_count = lax.axis_size("role")
    part = tokens // role_count
    role = lax.axis_index("role")
    own_part = lax.dynamic_slice_in_dim(prompt_latent, role * part, part, axis=0)
    gathered = own_part[None]
    for step in doublings(context_size):
        gathered = jnp.concatenate([gathered, swap(gathered, "ctx", step)], axis=0)
    other = swap(gathered[1:], "role", 1)
    far_first = jnp.where(role == 0, gathered[1:], other)
    far_second = jnp.where(role == 0, other, gathered[1:])
    shard_rows = jnp.concatenate(
        [prompt_latent[None], jnp.concatenate([far_first, far_second], axis=1)], axis=0
    ).reshape(context_size * tokens, prompt_latent.shape[1])
    sources = slot_ids ^ place
    block_pos = jnp.sum(
        jnp.where(sources[:, None] == slot_ids[None, :], block_order[None, :], 0), axis=1
    )
    key_pos = jnp.repeat(block_pos * tokens, tokens) + jnp.tile(jnp.arange(tokens), context_size)

    own_block = jnp.sum(jnp.where(slot_ids == place, block_order, 0))
    own_dest = jnp.sum(jnp.where(slot_ids == place, block_dest, 0))

    queries = absorbed(step_query, key_up)
    cache_scores = jnp.einsum(
        "sbhc,bpc->sbhp", queries, cache_latent, preferred_element_type=jnp.float32
    )
    cache_pos = place * cache_span + jnp.arange(cache_span)
    live_mask = jnp.broadcast_to(
        (cache_pos[None, :] < cache_length[:, None])[None, :, None, :], cache_scores.shape
    )
    handed_scores = jnp.einsum(
        "sbhc,pc->sbhp", queries, prompt_latent, preferred_element_type=jnp.float32
    )
    handed = jnp.broadcast_to(
        (jnp.arange(row_count) == own_dest)[None, :, None, None], handed_scores.shape
    )
    fresh_scores = jnp.einsum(
        "sbhc,ubc->sbhu", queries, step_latent, preferred_element_type=jnp.float32
    )
    step_ids = jnp.arange(step_count)
    order_mask = (step_ids[None, :] <= step_ids[:, None])[:, None, None, :] & (place == 0)
    order_mask = jnp.broadcast_to(order_mask, fresh_scores.shape)
    scores = jnp.concatenate([cache_scores, handed_scores, fresh_scores], axis=-1) * score_scale
    mask = jnp.concatenate([live_mask, handed, order_mask], axis=-1)
    scores = jnp.where(mask, scores, -1e30)
    highest = jnp.max(scores, axis=-1)
    weights = jnp.where(mask, jnp.exp(scores - highest[..., None]), 0.0)
    totals = jnp.sum(weights, axis=-1)
    weights = weights.astype(jnp.bfloat16)
    edge = cache_span + tokens
    summed = (
        jnp.einsum(
            "sbhp,bpc->sbhc",
            weights[..., :cache_span],
            cache_latent[..., :latent_width],
            preferred_element_type=jnp.float32,
        )
        + jnp.einsum(
            "sbhp,pc->sbhc",
            weights[..., cache_span:edge],
            prompt_latent[:, :latent_width],
            preferred_element_type=jnp.float32,
        )
        + jnp.einsum(
            "sbhu,ubc->sbhc",
            weights[..., edge:],
            step_latent[..., :latent_width],
            preferred_element_type=jnp.float32,
        )
    )
    attended_part = (summed / jnp.maximum(totals, 1e-30)[..., None]).astype(jnp.bfloat16)
    mixed = jnp.einsum(
        "sbhc,hcv->sbhv", attended_part, value_up, preferred_element_type=jnp.float32
    ).astype(jnp.bfloat16)
    running = (highest, totals, mixed)
    for step in doublings(context_size):
        stats = jnp.stack(running[:2])
        far_stats = swap(stats, "ctx", step)
        far_mixed = swap(running[2], "ctx", step)
        highest, totals, mixed = combine(running, (far_stats[0], far_stats[1], far_mixed))
        running = (highest, totals, mixed.astype(jnp.bfloat16))
    flat_heads = running[2].reshape(step_count * row_count, head_count * value_up.shape[2])
    share = jnp.dot(flat_heads, out_weight, preferred_element_type=jnp.float32)
    head_size = lax.axis_size("head")
    share = share.reshape(step_count * row_count, head_size, role_count, -1)
    for axis, place_dim, size in (("role", 2, role_count), ("head", 1, head_size)):
        index = lax.axis_index(axis)
        for step in reversed(doublings(size)):
            halves = share.shape[place_dim] // 2
            low = lax.slice_in_dim(share, 0, halves, axis=place_dim)
            high = lax.slice_in_dim(share, halves, 2 * halves, axis=place_dim)
            upper = (index & step) != 0
            keep = jnp.where(upper, high, low)
            give = jnp.where(upper, low, high)
            share = keep + swap(give, axis, step)
    step_out = share.reshape(step_count, row_count, -1).astype(jnp.bfloat16)

    query_pos = own_block * tokens + jnp.arange(tokens)
    row_pos = jnp.repeat(query_pos, head_count)
    query_rows = absorbed(prompt_query, key_up).reshape(tokens * head_count, -1)
    scores = (
        lax.dot_general(
            query_rows, shard_rows, (((1,), (1,)), ((), ())), preferred_element_type=jnp.float32
        )
        * score_scale
    )
    visible = key_pos[None, :] <= row_pos[:, None]
    scores = jnp.where(visible, scores, -1e30)
    peak_now = jnp.max(scores, axis=1)
    weights = jnp.where(visible, jnp.exp(scores - peak_now[:, None]), 0.0)
    totals = jnp.sum(weights, axis=1)
    summed = jnp.dot(
        weights.astype(jnp.bfloat16),
        shard_rows[:, :latent_width],
        preferred_element_type=jnp.float32,
    )
    attended = (
        (summed / totals[:, None]).astype(jnp.bfloat16).reshape(tokens, head_count, latent_width)
    )
    prompt_out = jnp.einsum(
        "thc,hcv->thv", attended, value_up, preferred_element_type=jnp.float32
    ).astype(jnp.bfloat16)
    prompt_out = prompt_out.reshape(tokens, head_count * value_up.shape[2])
    return (prompt_out, step_out)


def solution(mesh):
    return jax.shard_map(
        per_device,
        mesh=mesh,
        in_specs=(
            P(("groups", "ctx"), ("head", "role"), None),
            P(("groups", "ctx"), None),
            P("groups"),
            P(("head", "role"), None, None),
            P(("head", "role"), None, None),
            P(("head", "role"), "ctx"),
            P(None, "groups", ("head", "role"), None),
            P("groups", "ctx", None),
            P(None, "groups", None),
            P("groups"),
            P("groups"),
        ),
        out_specs=(
            P(("groups", "ctx"), ("head", "role")),
            P(None, "groups", ("ctx", "head", "role")),
        ),
        check_vma=False,
    )
```

```python
import functools
import math

import jax
import jax.numpy as jnp
from jax import lax
from jax.experimental import pallas as pl
from jax.experimental.pallas import tpu as pltpu
from jax.sharding import PartitionSpec as P

BF16 = jnp.bfloat16
F32 = jnp.float32
LANES = 128
HIDDEN = -1e30
FLOOR = -1e29
TINY = 1e-30
MIB = 1 << 20

VMEM = pl.BlockSpec(memory_space=pltpu.VMEM)
ANY = pl.BlockSpec(memory_space=pl.ANY)
NT = (((1,), (1,)), ((), ()))


def dot(left, right):
    return jnp.dot(left, right, preferred_element_type=F32)


def dot_nt(left, right):
    return lax.dot_general(left, right, NT, preferred_element_type=F32)


def doublings(size):
    steps = []
    step = 1
    while step < size:
        steps.append(step)
        step *= 2
    assert step == size
    return steps


def swap(value, axis, step):
    size = lax.axis_size(axis)
    return lax.ppermute(value, axis, [(i, i ^ step) for i in range(size)])


def in_hbm(value):
    return pltpu.with_memory_space_constraint(value, pltpu.HBM)


def in_vmem(value):
    return pltpu.with_memory_space_constraint(value, pltpu.VMEM)


def params(mib):
    return pltpu.CompilerParams(vmem_limit_bytes=mib * MIB)


def split_three(value):
    high = value.astype(BF16).astype(F32)
    rest = value - high
    middle = rest.astype(BF16).astype(F32)
    return high, middle, (rest - middle).astype(BF16).astype(F32)


def pick_piece(pieces, piece_ids):
    picked = pieces[-1]
    for index in reversed(range(len(pieces) - 1)):
        picked = jnp.where(piece_ids == index, pieces[index], picked)
    return picked


def step_kernel(
    rate,
    order_hbm,
    length_hbm,
    dest_hbm,
    query_hbm,
    key_up_hbm,
    cache_hbm,
    latent_hbm,
    fresh_hbm,
    value_up_hbm,
    prompt_hbm,
    weight_hbm,
    out_ref,
    key_up_ref,
    value_up_ref,
    latent_ref,
    prompt_ref,
    weight_ref,
    key_pos_ref,
    query_pos_ref,
    order_ref,
    length_ref,
    dest_ref,
    query_ref,
    cache_ref,
    fresh_ref,
    nope_ref,
    row_ref,
    extra_ref,
    mixed_ref,
    sems,
):
    steps, requests, heads, width = query_ref.shape
    nope, latent = key_up_ref.shape[1:]
    span = cache_ref.shape[2]
    tokens = latent_ref.shape[0]
    pairs = steps * requests
    rows = pairs * heads
    block = steps * heads
    place = lax.axis_index("ctx")
    role = lax.axis_index("role")

    copies = []

    def fetch(source, target):
        copies.append(pltpu.make_async_copy(source, target, sems.at[len(copies)]))
        copies[-1].start()
        return copies[-1]

    query_copy = fetch(query_hbm, query_ref)
    quarter = heads // 4
    key_up_copies = [
        fetch(key_up_hbm.at[at : at + quarter], key_up_ref.at[at : at + quarter])
        for at in range(0, heads, quarter)
    ]
    latent_copy = fetch(latent_hbm, latent_ref)
    fresh_copy = fetch(fresh_hbm, fresh_ref)
    scalar_copies = [
        fetch(length_hbm, length_ref),
        fetch(dest_hbm, dest_ref),
        fetch(order_hbm, order_ref),
    ]
    cache_copy = fetch(cache_hbm, cache_ref)
    value_up_copy = fetch(value_up_hbm, value_up_ref)
    prompt_copy = fetch(prompt_hbm, prompt_ref)
    weight_copy = fetch(weight_hbm.at[: weight_ref.shape[0]], weight_ref)

    query_copy.wait()
    query = query_ref[...].astype(F32)
    query = jnp.concatenate(
        [query[:, request].reshape(block, width) for request in range(requests)], axis=0
    )
    nope_ref[...] = query[:, :nope]
    rope = query[:, nope:]
    for head in range(heads):
        if head % quarter == 0:
            key_up_copies[head // quarter].wait()
        part = nope_ref[pl.ds(head, pairs, stride=heads), :].astype(BF16)
        lifted = dot(part, key_up_ref[head]).astype(BF16).astype(F32)
        for lane in range(0, latent, LANES):
            row_ref[lane // LANES, pl.ds(head, pairs, stride=heads), :] = lifted[
                :, lane : lane + LANES
            ]
    row_parts = [row_ref[index] for index in range(latent // LANES)] + [rope]
    query_rows = jnp.concatenate(row_parts, axis=1).astype(BF16)

    latent_copy.wait()
    fresh_copy.wait()
    extra_ref[:tokens, :] = latent_ref[...].astype(F32)
    for step in range(steps):
        extra_ref[tokens + step * requests : tokens + (step + 1) * requests, :] = fresh_ref[
            step
        ].astype(F32)
    extra = extra_ref[...].astype(BF16)
    more = dot_nt(query_rows, extra)
    for copy in scalar_copies:
        copy.wait()
    column = lax.broadcasted_iota(jnp.int32, more.shape, 1)
    row = lax.broadcasted_iota(jnp.int32, more.shape, 0)
    fresh_id = column - tokens
    seen = ((column < tokens) & (row // block == dest_ref[place])) | (
        (column >= tokens)
        & (fresh_id % requests == row // block)
        & (fresh_id // requests <= row // heads % steps)
        & (place == 0)
    )
    more = jnp.where(seen, more, HIDDEN)
    position = place * span + lax.broadcasted_iota(jnp.int32, (1, span), 1)
    cache_copy.wait()
    scores = [
        jnp.where(
            position < length_ref[request],
            dot(query_rows[request * block : (request + 1) * block], cache_ref[request]),
            HIDDEN,
        )
        for request in range(requests)
    ]
    scores = jnp.concatenate(scores, axis=0)
    high = jnp.maximum(
        jnp.max(scores, axis=1, keepdims=True), jnp.max(more, axis=1, keepdims=True)
    )
    high = jnp.maximum(high, FLOOR)
    weights = jnp.exp2((scores - high) * rate)
    more = jnp.exp2((more - high) * rate)
    total = jnp.sum(weights, axis=1, keepdims=True) + jnp.sum(more, axis=1, keepdims=True)
    weights = weights.astype(BF16)
    mixed = jnp.concatenate(
        [
            dot_nt(weights[request * block : (request + 1) * block], cache_ref[request, :latent])
            for request in range(requests)
        ],
        axis=0,
    )
    mixed = mixed + dot(more.astype(BF16), extra[:, :latent])
    mixed = mixed / jnp.maximum(total, TINY)
    for lane in range(0, latent, LANES):
        mixed_ref[lane // LANES] = mixed[:, lane : lane + LANES]
    high = jnp.broadcast_to(high, (rows, LANES))
    total = jnp.broadcast_to(total, (rows, LANES))

    value_up_copy.wait()
    value_width = value_up_ref.shape[2]
    for head in range(heads):
        parts = [
            mixed_ref[index, pl.ds(head, pairs, stride=heads), :]
            for index in range(latent // LANES)
        ]
        part = jnp.concatenate(parts, axis=1).astype(BF16)
        out_ref[:, head * value_width : (head + 1) * value_width] = dot(
            part, value_up_ref[head]
        ).astype(BF16)
    lane = lax.broadcasted_iota(jnp.int32, (rows, LANES), 1)
    head_of_row = lax.broadcasted_iota(jnp.int32, (rows, LANES), 0) % heads
    pieces = split_three(high) + split_three(total)
    packed = pick_piece(pieces, lane // heads)
    packed = jnp.where((lane % heads == head_of_row) & (lane < 6 * heads), packed, 0.0)
    packed = jnp.sum(packed.reshape(pairs, heads, LANES), axis=1)
    out_ref[:, heads * value_width :] = packed.astype(BF16)

    size = lax.axis_size("ctx")
    half = tokens // lax.axis_size("role")
    key_id = lax.broadcasted_iota(jnp.int32, key_pos_ref.shape, 1)
    near = 2 * tokens
    far = (size - 2) * half
    in_other = key_id >= near + far
    local = key_id - near - jnp.where(in_other, far, 0)
    is_near = key_id < near
    slot = jnp.where(is_near, key_id // tokens, 2 + local // half)
    base = jnp.where(
        is_near, key_id % tokens, local % half + half * jnp.where(in_other, 1 - role, role)
    )
    for index in range(size):
        base = base + jnp.where(slot == index, order_ref[place ^ index] * tokens, 0)
    key_pos_ref[...] = base
    query_pos_ref[...] = order_ref[place] * tokens + lax.broadcasted_iota(
        jnp.int32, query_pos_ref.shape, 0
    )
    prompt_copy.wait()
    weight_copy.wait()


def step_part(
    rate,
    early_rows,
    block_order,
    cache_length,
    block_dest,
    step_query,
    key_up,
    cache,
    latent,
    fresh,
    value_up,
    prompt_query,
    out_weight,
):
    steps, requests, heads, width = step_query.shape
    nope, latent_width = key_up.shape[1:]
    full = cache.shape[1]
    tokens = latent.shape[0]
    pairs = steps * requests
    rows = pairs * heads
    shape = pltpu.VMEM
    return pl.pallas_call(
        functools.partial(step_kernel, rate),
        out_shape=(
            shape((pairs, heads * value_up.shape[2] + LANES), BF16),
            shape(key_up.shape, BF16),
            shape(value_up.shape, BF16),
            shape(latent.shape, BF16),
            shape(prompt_query.shape, BF16),
            shape((early_rows, out_weight.shape[1]), BF16),
            shape((8, tokens * lax.axis_size("ctx")), jnp.int32),
            shape((tokens, LANES), jnp.int32),
        ),
        in_specs=[ANY] * 11,
        out_specs=[VMEM] * 8,
        scratch_shapes=[
            pltpu.SMEM(block_order.shape, jnp.int32),
            pltpu.SMEM(cache_length.shape, jnp.int32),
            pltpu.SMEM(block_dest.shape, jnp.int32),
            pltpu.VMEM(step_query.shape, BF16),
            pltpu.VMEM(cache.shape, BF16),
            pltpu.VMEM(fresh.shape, BF16),
            pltpu.VMEM((rows, nope), F32),
            pltpu.VMEM((latent_width // LANES, rows, LANES), F32),
            pltpu.VMEM((tokens + pairs, full), F32),
            pltpu.VMEM((latent_width // LANES, rows, LANES), F32),
            pltpu.SemaphoreType.DMA((14,)),
        ],
        compiler_params=params(24),
        cost_estimate=pl.CostEstimate(flops=10**9, bytes_accessed=10**7, transcendentals=10**5),
        name="step_part",
    )(
        *(
            in_hbm(value)
            for value in (
                block_order,
                cache_length,
                block_dest,
                step_query,
                key_up,
                cache,
                latent,
                fresh,
                value_up,
                prompt_query,
                out_weight,
            )
        )
    )


def read_stats(packed, heads):
    def piece(index):
        if index == 0:
            return packed
        return pltpu.roll(packed, LANES - index * heads, 1)

    return piece(0) + piece(1) + piece(2), piece(3) + piece(4) + piece(5)


def merge(rate, first_ref, second_ref, heads):
    split = first_ref.shape[1] - LANES
    value_width = split // heads
    high_a, total_a = read_stats(first_ref[:, split:].astype(F32), heads)
    high_b, total_b = read_stats(second_ref[:, split:].astype(F32), heads)
    high = jnp.maximum(high_a, high_b)
    share_a = total_a * jnp.exp2((high_a - high) * rate)
    share_b = total_b * jnp.exp2((high_b - high) * rate)
    total = share_a + share_b
    safe = jnp.maximum(total, TINY)
    share_a = share_a / safe
    share_b = share_b / safe
    merged = []
    for head in range(heads):
        at = slice(head * value_width, (head + 1) * value_width)
        merged.append(
            (
                first_ref[:, at].astype(F32) * share_a[:, head : head + 1]
                + second_ref[:, at].astype(F32) * share_b[:, head : head + 1]
            ).astype(BF16)
        )
    return merged, high, total


def merge_kernel(rate, heads, first_ref, second_ref, out_ref):
    merged, high, total = merge(rate, first_ref, second_ref, heads)
    value_width = merged[0].shape[1]
    for head in range(heads):
        out_ref[:, head * value_width : (head + 1) * value_width] = merged[head]
    pieces = split_three(high) + split_three(total)
    lane = lax.broadcasted_iota(jnp.int32, high.shape, 1)
    moved = [p if i == 0 else pltpu.roll(p, i * heads, 1) for i, p in enumerate(pieces)]
    packed = jnp.where(lane < 6 * heads, pick_piece(moved, lane // heads), 0.0)
    out_ref[:, heads * value_width :] = packed.astype(BF16)


def merge_parts(rate, heads, first, second):
    return pl.pallas_call(
        functools.partial(merge_kernel, rate, heads),
        out_shape=pltpu.VMEM(first.shape, BF16),
        in_specs=[VMEM] * 2,
        out_specs=VMEM,
        compiler_params=params(2),
        cost_estimate=pl.CostEstimate(flops=10**5, bytes_accessed=2 * 10**5, transcendentals=10**4),
        name="merge_parts",
    )(in_vmem(first), in_vmem(second))


def join_kernel(half, first_ref, second_ref, out_ref):
    rows = first_ref.shape[0]
    if half:
        role = lax.axis_index("role")
        for index in range(rows // half):

            @pl.when(role == index)
            def _():
                at = slice(index * half, (index + 1) * half)
                out_ref[:half, :] = first_ref[at, :]
                out_ref[half:, :] = second_ref[at, :]
    else:
        out_ref[:rows, :] = first_ref[...]
        out_ref[rows:, :] = second_ref[...]


def join_rows(half, first, second):
    rows, full = first.shape
    return pl.pallas_call(
        functools.partial(join_kernel, half),
        out_shape=pltpu.VMEM((2 * (half or rows), full), BF16),
        in_specs=[VMEM] * 2,
        out_specs=VMEM,
        compiler_params=params(1),
        cost_estimate=pl.CostEstimate(flops=10**4, bytes_accessed=2 * 10**5, transcendentals=0),
        name="join_rows",
    )(in_vmem(first), in_vmem(second))


def finish_kernel(
    rate, heads, parts, first_ref, second_ref, early_ref, late_ref, keep_ref, give_ref
):
    merged, _, _ = merge(rate, first_ref, second_ref, heads)
    rows = jnp.concatenate(merged, axis=1)
    early = early_ref.shape[0]
    product = dot(rows[:, :early], early_ref[...]) + dot(rows[:, early:], late_ref[...])
    width = product.shape[1] // parts
    upper = lax.axis_index("role") == 1
    for index in range(parts // 2):
        low, high = (
            product[:, part * width : (part + 1) * width] for part in (2 * index, 2 * index + 1)
        )
        keep_ref[index] = jnp.where(upper, high, low)
        give_ref[index] = jnp.where(upper, low, high).astype(BF16)


def finish_steps(rate, heads, parts, first, second, early, late):
    pairs = first.shape[0]
    shape = (parts // 2, pairs, early.shape[1] // parts)
    return pl.pallas_call(
        functools.partial(finish_kernel, rate, heads, parts),
        out_shape=(pltpu.VMEM(shape, F32), pltpu.VMEM(shape, BF16)),
        in_specs=[VMEM] * 4,
        out_specs=[VMEM] * 2,
        compiler_params=params(4),
        cost_estimate=pl.CostEstimate(
            flops=5 * 10**8, bytes_accessed=8 * 10**6, transcendentals=10**4
        ),
        name="finish_steps",
    )(*(in_vmem(v) for v in (first, second, early, late)))


def fold_kernel(step, keep_ref, received_ref, new_keep_ref, give_ref):
    share = keep_ref[...] + received_ref[...].astype(F32)
    middle = share.shape[0] // 2
    upper = lax.axis_index("head") & step != 0
    new_keep_ref[...] = jnp.where(upper, share[middle:], share[:middle])
    give_ref[...] = jnp.where(upper, share[:middle], share[middle:]).astype(BF16)


def fold_steps(step, keep, received):
    shape = (keep.shape[0] // 2, *keep.shape[1:])
    return pl.pallas_call(
        functools.partial(fold_kernel, step),
        out_shape=(pltpu.VMEM(shape, F32), pltpu.VMEM(shape, BF16)),
        in_specs=[VMEM] * 2,
        out_specs=[VMEM] * 2,
        compiler_params=params(1),
        cost_estimate=pl.CostEstimate(flops=10**5, bytes_accessed=10**5, transcendentals=0),
        name="fold_steps",
    )(in_vmem(keep), in_vmem(received))


def sum_kernel(keep_ref, received_ref, out_ref):
    share = keep_ref[0] + received_ref[0].astype(F32)
    steps, requests, _ = out_ref.shape
    for step in range(steps):
        rows = [share[at : at + 1] for at in range(step, steps * requests, steps)]
        out_ref[step] = jnp.concatenate(rows, axis=0).astype(BF16)


def sum_steps(steps, keep, received):
    pairs, width = keep.shape[1:]
    return pl.pallas_call(
        sum_kernel,
        out_shape=jax.ShapeDtypeStruct((steps, pairs // steps, width), BF16),
        in_specs=[VMEM] * 2,
        out_specs=VMEM,
        compiler_params=params(1),
        cost_estimate=pl.CostEstimate(flops=10**5, bytes_accessed=10**5, transcendentals=0),
        name="sum_steps",
    )(in_vmem(keep), in_vmem(received))


def lift_kernel(query_ref, key_up_ref, weight_hbm, row_ref, weight_ref, nope_ref, rope_ref, sem):
    tokens, heads, width = query_ref.shape
    nope, latent = key_up_ref.shape[1:]
    skipped = weight_hbm.shape[0] - weight_ref.shape[0]
    copy = pltpu.make_async_copy(weight_hbm.at[skipped:], weight_ref, sem)
    copy.start()
    nope_ref[...] = query_ref[:, :, :nope].astype(F32).reshape(tokens * heads, nope)
    rope_ref[:, : width - nope] = (
        query_ref[:, :, nope:].astype(F32).reshape(tokens * heads, width - nope)
    )
    for head in range(heads):
        at = slice(head * tokens, (head + 1) * tokens)
        part = nope_ref[pl.ds(head, tokens, stride=heads), :].astype(BF16)
        row_ref[at, :latent] = dot(part, key_up_ref[head]).astype(BF16)
        rope = rope_ref[pl.ds(head, tokens, stride=heads), :]
        row_ref[at, latent:] = rope[:, : width - nope].astype(BF16)
    copy.wait()


def prompt_lift(prompt_query, key_up, out_weight, late_rows):
    tokens, heads, width = prompt_query.shape
    nope, latent_width = key_up.shape[1:]
    rows = tokens * heads
    shape = pltpu.VMEM
    return pl.pallas_call(
        lift_kernel,
        out_shape=(
            shape((rows, latent_width + width - nope), BF16),
            shape((late_rows, out_weight.shape[1]), BF16),
        ),
        in_specs=[VMEM] * 2 + [ANY],
        out_specs=[VMEM] * 2,
        scratch_shapes=[
            pltpu.VMEM((rows, nope), F32),
            pltpu.VMEM((rows, LANES), F32),
            pltpu.SemaphoreType.DMA,
        ],
        compiler_params=params(8),
        cost_estimate=pl.CostEstimate(
            flops=3 * 10**8, bytes_accessed=6 * 10**6, transcendentals=0
        ),
        name="prompt_lift",
    )(in_vmem(prompt_query), in_vmem(key_up), in_hbm(out_weight))


def attend(rate, group, heads, row_ref, key_ref, key_pos_ref, query_pos_ref, value_up_ref, put):
    tokens = query_pos_ref.shape[0]
    count = key_ref.shape[0]
    latent = value_up_ref.shape[1]
    visible = (key_pos_ref[:1, :] <= query_pos_ref[:, :1])[None]
    for first in range(heads.start, heads.stop, group):
        at = slice(first * tokens, (first + group) * tokens)
        scores = dot_nt(row_ref[at, :], key_ref[...])
        scores = jnp.where(visible, scores.reshape(group, tokens, count), HIDDEN)
        scores = scores.reshape(group * tokens, count)
        weights = jnp.exp2((scores - jnp.max(scores, axis=1, keepdims=True)) * rate)
        total = jnp.sum(weights, axis=1, keepdims=True)
        mixed = dot(weights.astype(BF16), key_ref[:, :latent])
        mixed = (mixed / total).astype(BF16)
        for index in range(group):
            put(
                first + index,
                dot(
                    mixed[index * tokens : (index + 1) * tokens], value_up_ref[first + index]
                ).astype(BF16),
            )


def front_kernel(rate, group, heads, skipped, *refs):
    row_ref, *part_refs = refs[: 1 + len(skipped)]
    key_pos_ref, query_pos_ref, value_up_ref, out_ref, key_ref = refs[1 + len(skipped) :]
    at = 0
    for part_ref, skip in zip(part_refs, skipped):
        count = part_ref.shape[0] - skip
        key_ref[at : at + count, :] = part_ref[skip:, :]
        at += count
    assert at == key_ref.shape[0]
    width = value_up_ref.shape[2]

    def put(head, value):
        out_ref[:, head * width : (head + 1) * width] = value

    attend(
        rate, group, heads, row_ref, key_ref, key_pos_ref, query_pos_ref, value_up_ref, put
    )


def prompt_front(rate, group, heads, rows, parts, key_pos, query_pos, value_up):
    tokens = query_pos.shape[0]
    shape = pltpu.VMEM
    return pl.pallas_call(
        functools.partial(front_kernel, rate, group, heads, [skip for _, skip in parts]),
        out_shape=(
            shape((tokens, len(heads) * value_up.shape[2]), BF16),
            shape((key_pos.shape[1], rows.shape[1]), BF16),
        ),
        in_specs=[VMEM] * (4 + len(parts)),
        out_specs=[VMEM] * 2,
        compiler_params=params(16),
        cost_estimate=pl.CostEstimate(
            flops=8 * 10**8, bytes_accessed=6 * 10**6, transcendentals=3 * 10**5
        ),
        name="prompt_front",
    )(*(in_vmem(v) for v in (rows, *(part for part, _ in parts), key_pos, query_pos, value_up)))


def back_kernel(
    rate,
    group,
    heads,
    row_ref,
    key_ref,
    key_pos_ref,
    query_pos_ref,
    value_up_ref,
    front_ref,
    out_hbm,
    back_ref,
    sems,
):
    width = value_up_ref.shape[2]
    edge = heads.start * width
    copies = [pltpu.make_async_copy(front_ref, out_hbm.at[:, :edge], sems.at[0])]
    copies[0].start()

    def put(head, value):
        at = (head - heads.start) * width
        back_ref[:, at : at + width] = value
        if (head - heads.start + 1) % group == 0:
            start = at + width - group * width
            copies.append(
                pltpu.make_async_copy(
                    back_ref.at[:, start : at + width],
                    out_hbm.at[:, edge + start : edge + at + width],
                    sems.at[len(copies)],
                )
            )
            copies[-1].start()

    attend(
        rate, group, heads, row_ref, key_ref, key_pos_ref, query_pos_ref, value_up_ref, put
    )
    for copy in copies:
        copy.wait()


def prompt_back(rate, group, heads, rows, keys, key_pos, query_pos, value_up, front):
    tokens = query_pos.shape[0]
    width = value_up.shape[2]
    return pl.pallas_call(
        functools.partial(back_kernel, rate, group, heads),
        out_shape=jax.ShapeDtypeStruct((tokens, heads.stop * width), BF16),
        in_specs=[VMEM] * 6,
        out_specs=ANY,
        scratch_shapes=[
            pltpu.VMEM((tokens, len(heads) * width), BF16),
            pltpu.SemaphoreType.DMA((1 + len(heads) // group,)),
        ],
        compiler_params=params(16),
        cost_estimate=pl.CostEstimate(
            flops=8 * 10**8, bytes_accessed=6 * 10**6, transcendentals=3 * 10**5
        ),
        name="prompt_back",
    )(*(in_vmem(v) for v in (rows, keys, key_pos, query_pos, value_up, front)))


def per_device(
    prompt_query,
    prompt_latent,
    block_order,
    key_up,
    value_up,
    out_weight,
    step_query,
    cache_latent,
    step_latent,
    cache_length,
    block_dest,
):
    tokens, heads, width = prompt_query.shape
    rate = width ** (-0.5) * math.log2(math.e)
    context_size = lax.axis_size("ctx")
    steps = step_query.shape[0]
    head_size = lax.axis_size("head")
    role_size = lax.axis_size("role")
    contracted = out_weight.shape[0]
    early_rows = contracted // 2

    rounds = doublings(context_size)
    near = swap(prompt_latent, "ctx", rounds[0])
    (
        running,
        key_up,
        value_up,
        latent,
        prompt_query,
        early_weight,
        key_pos,
        query_pos,
    ) = step_part(
        rate,
        early_rows,
        block_order,
        cache_length,
        block_dest,
        step_query,
        key_up,
        jnp.swapaxes(cache_latent, 1, 2),
        prompt_latent,
        step_latent,
        value_up,
        prompt_query,
        out_weight,
    )
    rows, late_weight = prompt_lift(prompt_query, key_up, out_weight, contracted - early_rows)
    sent = join_rows(tokens // role_size, latent, near)
    for step in rounds:
        far_running = swap(running, "ctx", step)
        if step == rounds[-1]:
            break
        running = merge_parts(rate, heads, running, far_running)
    for step in rounds[1:]:
        received = swap(sent, "ctx", step)
        if step == rounds[-1]:
            break
        sent = join_rows(None, sent, received)
    keep, give = finish_steps(
        rate, heads, head_size * role_size, running, far_running, early_weight, late_weight
    )
    same = [(sent, 2 * tokens // role_size), (received, 0)]
    same = [(part, skip) for part, skip in same if part.shape[0] > skip]
    parts = [(latent, 0), (near, 0)] + same
    parts += [(swap(part, "role", 1), skip) for part, skip in same]
    group = 4 if heads % 8 == 0 else 1
    middle = heads // 2
    front, keys = prompt_front(
        rate, group, range(middle), rows, parts, key_pos, query_pos, value_up
    )
    prompt_out = prompt_back(
        rate, group, range(middle, heads), rows, keys, key_pos, query_pos, value_up, front
    )
    partial = swap(give, "role", 1)
    for step in reversed(doublings(head_size)):
        keep, give = fold_steps(step, keep, partial)
        partial = swap(give, "head", step)
    step_out = sum_steps(steps, keep, partial)
    return (prompt_out, step_out)


def solution(mesh):
    return jax.shard_map(
        per_device,
        mesh=mesh,
        in_specs=(
            P(("groups", "ctx"), ("head", "role"), None),
            P(("groups", "ctx"), None),
            P("groups"),
            P(("head", "role"), None, None),
            P(("head", "role"), None, None),
            P(("head", "role"), "ctx"),
            P(None, "groups", ("head", "role"), None),
            P("groups", "ctx", None),
            P(None, "groups", None),
            P("groups"),
            P("groups"),
        ),
        out_specs=(
            P(("groups", "ctx"), ("head", "role")),
            P(None, "groups", ("ctx", "head", "role")),
        ),
        check_vma=False,
    )
```

```python
import functools
import math

import jax
import jax.numpy as jnp
from jax import lax
from jax.experimental import pallas as pl
from jax.experimental.pallas import tpu as pltpu
from jax.sharding import PartitionSpec as P


BF16 = jnp.bfloat16
F32 = jnp.float32
LANES = 128
HIDDEN = -1e30
FLOOR = -1e29
TINY = 1e-30
MIB = 1 << 20

VMEM = pl.BlockSpec(memory_space=pltpu.VMEM)
ANY = pl.BlockSpec(memory_space=pl.ANY)
NT = (((1,), (1,)), ((), ()))


def dot(left, right):
    return jnp.dot(left, right, preferred_element_type=F32)


def dot_nt(left, right):
    return lax.dot_general(left, right, NT, preferred_element_type=F32)


def doublings(size):
    steps = []
    step = 1
    while step < size:
        steps.append(step)
        step *= 2
    assert step == size
    return steps


def swap(value, axis, step):
    size = lax.axis_size(axis)
    return lax.ppermute(value, axis, [(i, i ^ step) for i in range(size)])


def in_hbm(value):
    return pltpu.with_memory_space_constraint(value, pltpu.HBM)


def in_vmem(value):
    return pltpu.with_memory_space_constraint(value, pltpu.VMEM)


def params(mib):
    return pltpu.CompilerParams(vmem_limit_bytes=mib * MIB)


def split_three(value):
    high = value.astype(BF16).astype(F32)
    rest = value - high
    middle = rest.astype(BF16).astype(F32)
    return high, middle, (rest - middle).astype(BF16).astype(F32)


def pick_piece(pieces, piece_ids):
    picked = pieces[-1]
    for index in reversed(range(len(pieces) - 1)):
        picked = jnp.where(piece_ids == index, pieces[index], picked)
    return picked


def step_kernel(
    rate,
    order_hbm,
    length_hbm,
    dest_hbm,
    query_hbm,
    key_up_hbm,
    cache_hbm,
    latent_hbm,
    fresh_hbm,
    value_up_hbm,
    prompt_hbm,
    weight_hbm,
    out_ref,
    key_up_ref,
    value_up_ref,
    latent_ref,
    prompt_ref,
    weight_ref,
    key_pos_ref,
    query_pos_ref,
    order_ref,
    length_ref,
    dest_ref,
    query_ref,
    cache_ref,
    fresh_ref,
    nope_ref,
    row_ref,
    extra_ref,
    mixed_ref,
    sems,
):
    steps, requests, heads, width = query_ref.shape
    nope, latent = key_up_ref.shape[1:]
    span = cache_ref.shape[2]
    tokens = latent_ref.shape[0]
    pairs = steps * requests
    rows = pairs * heads
    block = steps * heads
    place = lax.axis_index("ctx")

    copies = []

    def fetch(source, target):
        copies.append(pltpu.make_async_copy(source, target, sems.at[len(copies)]))
        copies[-1].start()
        return copies[-1]

    query_copy = fetch(query_hbm, query_ref)
    quarter = heads // 4
    key_up_copies = [
        fetch(key_up_hbm.at[at : at + quarter], key_up_ref.at[at : at + quarter])
        for at in range(0, heads, quarter)
    ]
    latent_copy = fetch(latent_hbm, latent_ref)
    fresh_copy = fetch(fresh_hbm, fresh_ref)
    scalar_copies = [
        fetch(length_hbm, length_ref),
        fetch(dest_hbm, dest_ref),
        fetch(order_hbm, order_ref),
    ]
    cache_copy = fetch(cache_hbm, cache_ref)
    value_up_copy = fetch(value_up_hbm, value_up_ref)
    prompt_copy = fetch(prompt_hbm, prompt_ref)
    weight_copy = fetch(weight_hbm.at[: weight_ref.shape[0]], weight_ref)

    query_copy.wait()
    query = query_ref[...].astype(F32)
    query = jnp.concatenate(
        [query[:, request].reshape(block, width) for request in range(requests)], axis=0
    )
    nope_ref[...] = query[:, :nope]
    rope = query[:, nope:]
    for head in range(heads):
        if head % quarter == 0:
            key_up_copies[head // quarter].wait()
        part = nope_ref[pl.ds(head, pairs, stride=heads), :].astype(BF16)
        lifted = dot(part, key_up_ref[head]).astype(BF16).astype(F32)
        for lane in range(0, latent, LANES):
            row_ref[lane // LANES, pl.ds(head, pairs, stride=heads), :] = lifted[
                :, lane : lane + LANES
            ]
    row_parts = [row_ref[index] for index in range(latent // LANES)] + [rope]
    query_rows = jnp.concatenate(row_parts, axis=1).astype(BF16)

    latent_copy.wait()
    fresh_copy.wait()
    extra_ref[:tokens, :] = latent_ref[...].astype(F32)
    for step in range(steps):
        extra_ref[tokens + step * requests : tokens + (step + 1) * requests, :] = fresh_ref[
            step
        ].astype(F32)
    extra = extra_ref[...].astype(BF16)
    more = dot_nt(query_rows, extra)
    for copy in scalar_copies:
        copy.wait()
    column = lax.broadcasted_iota(jnp.int32, more.shape, 1)
    row = lax.broadcasted_iota(jnp.int32, more.shape, 0)
    fresh_id = column - tokens
    seen = ((column < tokens) & (row // block == dest_ref[place])) | (
        (column >= tokens)
        & (fresh_id % requests == row // block)
        & (fresh_id // requests <= row // heads % steps)
        & (place == 0)
    )
    more = jnp.where(seen, more, HIDDEN)
    position = place * span + lax.broadcasted_iota(jnp.int32, (1, span), 1)
    cache_copy.wait()
    scores = [
        jnp.where(
            position < length_ref[request],
            dot(query_rows[request * block : (request + 1) * block], cache_ref[request]),
            HIDDEN,
        )
        for request in range(requests)
    ]
    scores = jnp.concatenate(scores, axis=0)
    high = jnp.maximum(
        jnp.max(scores, axis=1, keepdims=True), jnp.max(more, axis=1, keepdims=True)
    )
    high = jnp.maximum(high, FLOOR)
    weights = jnp.exp2((scores - high) * rate)
    more = jnp.exp2((more - high) * rate)
    total = jnp.sum(weights, axis=1, keepdims=True) + jnp.sum(more, axis=1, keepdims=True)
    weights = weights.astype(BF16)
    mixed = jnp.concatenate(
        [
            dot_nt(weights[request * block : (request + 1) * block], cache_ref[request, :latent])
            for request in range(requests)
        ],
        axis=0,
    )
    mixed = mixed + dot(more.astype(BF16), extra[:, :latent])
    mixed = mixed / jnp.maximum(total, TINY)
    for lane in range(0, latent, LANES):
        mixed_ref[lane // LANES] = mixed[:, lane : lane + LANES]
    high = jnp.broadcast_to(high, (rows, LANES))
    total = jnp.broadcast_to(total, (rows, LANES))

    value_up_copy.wait()
    value_width = value_up_ref.shape[2]
    for head in range(heads):
        parts = [
            mixed_ref[index, pl.ds(head, pairs, stride=heads), :]
            for index in range(latent // LANES)
        ]
        part = jnp.concatenate(parts, axis=1).astype(BF16)
        out_ref[:, head * value_width : (head + 1) * value_width] = dot(
            part, value_up_ref[head]
        ).astype(BF16)
    lane = lax.broadcasted_iota(jnp.int32, (rows, LANES), 1)
    head_of_row = lax.broadcasted_iota(jnp.int32, (rows, LANES), 0) % heads
    pieces = split_three(high) + split_three(total)
    packed = pick_piece(pieces, lane // heads)
    packed = jnp.where((lane % heads == head_of_row) & (lane < 6 * heads), packed, 0.0)
    packed = jnp.sum(packed.reshape(pairs, heads, LANES), axis=1)
    out_ref[:, heads * value_width :] = packed.astype(BF16)

    key_id = lax.broadcasted_iota(jnp.int32, key_pos_ref.shape, 1)
    base = key_id
    for slot in range(key_pos_ref.shape[1] // tokens):
        move = (order_ref[place ^ slot] - slot) * tokens
        base = base + jnp.where(key_id // tokens == slot, move, 0)
    key_pos_ref[...] = base
    query_pos_ref[...] = order_ref[place] * tokens + lax.broadcasted_iota(
        jnp.int32, query_pos_ref.shape, 0
    )
    prompt_copy.wait()
    weight_copy.wait()


def step_part(
    rate,
    early_rows,
    block_order,
    cache_length,
    block_dest,
    step_query,
    key_up,
    cache,
    latent,
    fresh,
    value_up,
    prompt_query,
    out_weight,
):
    steps, requests, heads, _ = step_query.shape
    nope, latent_width = key_up.shape[1:]
    full = cache.shape[1]
    tokens = latent.shape[0]
    pairs = steps * requests
    rows = pairs * heads
    shape = pltpu.VMEM
    return pl.pallas_call(
        functools.partial(step_kernel, rate),
        out_shape=(
            shape((pairs, heads * value_up.shape[2] + LANES), BF16),
            shape(key_up.shape, BF16),
            shape(value_up.shape, BF16),
            shape(latent.shape, BF16),
            shape(prompt_query.shape, BF16),
            shape((early_rows, out_weight.shape[1]), BF16),
            shape((8, tokens * lax.axis_size("ctx")), jnp.int32),
            shape((tokens, LANES), jnp.int32),
        ),
        in_specs=[ANY] * 11,
        out_specs=[VMEM] * 8,
        scratch_shapes=[
            pltpu.SMEM(block_order.shape, jnp.int32),
            pltpu.SMEM(cache_length.shape, jnp.int32),
            pltpu.SMEM(block_dest.shape, jnp.int32),
            pltpu.VMEM(step_query.shape, BF16),
            pltpu.VMEM(cache.shape, BF16),
            pltpu.VMEM(fresh.shape, BF16),
            pltpu.VMEM((rows, nope), F32),
            pltpu.VMEM((latent_width // LANES, rows, LANES), F32),
            pltpu.VMEM((tokens + pairs, full), F32),
            pltpu.VMEM((latent_width // LANES, rows, LANES), F32),
            pltpu.SemaphoreType.DMA((14,)),
        ],
        compiler_params=params(24),
        cost_estimate=pl.CostEstimate(flops=10**9, bytes_accessed=10**7, transcendentals=10**5),
        name="step_part",
    )(
        *(
            in_hbm(value)
            for value in (
                block_order,
                cache_length,
                block_dest,
                step_query,
                key_up,
                cache,
                latent,
                fresh,
                value_up,
                prompt_query,
                out_weight,
            )
        )
    )


def read_stats(packed, heads):
    def piece(index):
        if index == 0:
            return packed
        return pltpu.roll(packed, LANES - index * heads, 1)

    return piece(0) + piece(1) + piece(2), piece(3) + piece(4) + piece(5)


def merge(rate, first_ref, second_ref, heads):
    split = first_ref.shape[1] - LANES
    value_width = split // heads
    high_a, total_a = read_stats(first_ref[:, split:].astype(F32), heads)
    high_b, total_b = read_stats(second_ref[:, split:].astype(F32), heads)
    high = jnp.maximum(high_a, high_b)
    share_a = total_a * jnp.exp2((high_a - high) * rate)
    share_b = total_b * jnp.exp2((high_b - high) * rate)
    total = share_a + share_b
    safe = jnp.maximum(total, TINY)
    share_a = share_a / safe
    share_b = share_b / safe
    merged = []
    for head in range(heads):
        at = slice(head * value_width, (head + 1) * value_width)
        merged.append(
            (
                first_ref[:, at].astype(F32) * share_a[:, head : head + 1]
                + second_ref[:, at].astype(F32) * share_b[:, head : head + 1]
            ).astype(BF16)
        )
    return merged, high, total


def merge_kernel(rate, heads, first_ref, second_ref, out_ref):
    merged, high, total = merge(rate, first_ref, second_ref, heads)
    value_width = merged[0].shape[1]
    for head in range(heads):
        out_ref[:, head * value_width : (head + 1) * value_width] = merged[head]
    pieces = split_three(high) + split_three(total)
    lane = lax.broadcasted_iota(jnp.int32, high.shape, 1)
    moved = [p if i == 0 else pltpu.roll(p, i * heads, 1) for i, p in enumerate(pieces)]
    packed = jnp.where(lane < 6 * heads, pick_piece(moved, lane // heads), 0.0)
    out_ref[:, heads * value_width :] = packed.astype(BF16)


def merge_parts(rate, heads, first, second):
    return pl.pallas_call(
        functools.partial(merge_kernel, rate, heads),
        out_shape=pltpu.VMEM(first.shape, BF16),
        in_specs=[VMEM] * 2,
        out_specs=VMEM,
        compiler_params=params(2),
        cost_estimate=pl.CostEstimate(flops=10**5, bytes_accessed=2 * 10**5, transcendentals=10**4),
        name="merge_parts",
    )(in_vmem(first), in_vmem(second))


def halves_kernel(first_ref, second_ref, out_ref):
    half = first_ref.shape[0] // 2
    for index in range(2):

        @pl.when(lax.axis_index("role") == index)
        def _():
            at = slice(index * half, (index + 1) * half)
            out_ref[:half, :] = first_ref[at, :]
            out_ref[half:, :] = second_ref[at, :]


def gather_kernel(own_ref, far_ref, mine_ref, other_ref, out_ref):
    tokens = own_ref.shape[0]
    half = tokens // 2
    out_ref[:tokens, :] = own_ref[...]
    out_ref[2 * tokens : 3 * tokens, :] = far_ref[...]
    for index, sources in enumerate(((mine_ref, other_ref), (other_ref, mine_ref))):

        @pl.when(lax.axis_index("role") == index)
        def _():
            for part, source in enumerate(sources):
                for slot in range(2):
                    at = (2 * slot + 1) * tokens + part * half
                    out_ref[at : at + half, :] = source[slot * half : (slot + 1) * half, :]


def half_kernel(keys_ref, out_ref):
    rows = out_ref.shape[0]
    for index in range(2):

        @pl.when(lax.axis_index("role") == index)
        def _():
            out_ref[...] = keys_ref[index * rows : (index + 1) * rows, :]


def extend_kernel(keys_ref, mine_ref, other_ref, out_ref):
    rows = keys_ref.shape[0]
    half = mine_ref.shape[0]
    out_ref[:rows, :] = keys_ref[...]
    for index, sources in enumerate(((mine_ref, other_ref), (other_ref, mine_ref))):

        @pl.when(lax.axis_index("role") == index)
        def _():
            out_ref[rows : rows + half, :] = sources[0][...]
            out_ref[rows + half :, :] = sources[1][...]


def move_rows(body, rows, *sources):
    return pl.pallas_call(
        body,
        out_shape=pltpu.VMEM((rows, sources[0].shape[1]), BF16),
        in_specs=[VMEM] * len(sources),
        out_specs=VMEM,
        compiler_params=params(1),
        cost_estimate=pl.CostEstimate(flops=10**4, bytes_accessed=4 * 10**5, transcendentals=0),
    )(*(in_vmem(source) for source in sources))


def finish_kernel(
    rate, heads, parts, first_ref, second_ref, early_ref, late_ref, keep_ref, give_ref
):
    merged, _, _ = merge(rate, first_ref, second_ref, heads)
    rows = jnp.concatenate(merged, axis=1)
    early = early_ref.shape[0]
    product = dot(rows[:, :early], early_ref[...]) + dot(rows[:, early:], late_ref[...])
    width = product.shape[1] // parts
    upper = lax.axis_index("role") == 1
    for index in range(parts // 2):
        low, high = (
            product[:, part * width : (part + 1) * width] for part in (2 * index, 2 * index + 1)
        )
        keep_ref[index] = jnp.where(upper, high, low)
        give_ref[index] = jnp.where(upper, low, high).astype(BF16)


def finish_steps(rate, heads, parts, first, second, early, late):
    pairs = first.shape[0]
    shape = (parts // 2, pairs, early.shape[1] // parts)
    return pl.pallas_call(
        functools.partial(finish_kernel, rate, heads, parts),
        out_shape=(pltpu.VMEM(shape, F32), pltpu.VMEM(shape, BF16)),
        in_specs=[VMEM] * 4,
        out_specs=[VMEM] * 2,
        compiler_params=params(4),
        cost_estimate=pl.CostEstimate(
            flops=5 * 10**8, bytes_accessed=8 * 10**6, transcendentals=10**4
        ),
        name="finish_steps",
    )(*(in_vmem(v) for v in (first, second, early, late)))


def fold_kernel(step, keep_ref, received_ref, new_keep_ref, give_ref):
    share = keep_ref[...] + received_ref[...].astype(F32)
    middle = share.shape[0] // 2
    upper = lax.axis_index("head") & step != 0
    new_keep_ref[...] = jnp.where(upper, share[middle:], share[:middle])
    give_ref[...] = jnp.where(upper, share[:middle], share[middle:]).astype(BF16)


def fold_steps(step, keep, received):
    shape = (keep.shape[0] // 2, *keep.shape[1:])
    return pl.pallas_call(
        functools.partial(fold_kernel, step),
        out_shape=(pltpu.VMEM(shape, F32), pltpu.VMEM(shape, BF16)),
        in_specs=[VMEM] * 2,
        out_specs=[VMEM] * 2,
        compiler_params=params(1),
        cost_estimate=pl.CostEstimate(flops=10**5, bytes_accessed=10**5, transcendentals=0),
        name="fold_steps",
    )(in_vmem(keep), in_vmem(received))


def sum_kernel(keep_ref, received_ref, out_ref):
    share = keep_ref[0] + received_ref[0].astype(F32)
    steps, requests, _ = out_ref.shape
    for step in range(steps):
        rows = [share[at : at + 1] for at in range(step, steps * requests, steps)]
        out_ref[step] = jnp.concatenate(rows, axis=0).astype(BF16)


def sum_steps(steps, keep, received):
    pairs, width = keep.shape[1:]
    return pl.pallas_call(
        sum_kernel,
        out_shape=jax.ShapeDtypeStruct((steps, pairs // steps, width), BF16),
        in_specs=[VMEM] * 2,
        out_specs=VMEM,
        compiler_params=params(1),
        cost_estimate=pl.CostEstimate(flops=10**5, bytes_accessed=10**5, transcendentals=0),
        name="sum_steps",
    )(in_vmem(keep), in_vmem(received))


def lift_kernel(heads, query_ref, key_up_ref, row_ref, nope_ref, rope_ref):
    tokens, every, width = query_ref.shape
    nope, latent = key_up_ref.shape[1:]
    nope_ref[...] = query_ref[:, :, :nope].astype(F32).reshape(tokens * every, nope)
    rope_ref[:, : width - nope] = (
        query_ref[:, :, nope:].astype(F32).reshape(tokens * every, width - nope)
    )
    for index, head in enumerate(heads):
        at = slice(index * tokens, (index + 1) * tokens)
        part = nope_ref[pl.ds(head, tokens, stride=every), :].astype(BF16)
        row_ref[at, :latent] = dot(part, key_up_ref[head]).astype(BF16)
        rope = rope_ref[pl.ds(head, tokens, stride=every), :]
        row_ref[at, latent:] = rope[:, : width - nope].astype(BF16)


def prompt_lift(heads, prompt_query, key_up):
    tokens, every, width = prompt_query.shape
    nope, latent_width = key_up.shape[1:]
    return pl.pallas_call(
        functools.partial(lift_kernel, heads),
        out_shape=pltpu.VMEM((tokens * len(heads), latent_width + width - nope), BF16),
        in_specs=[VMEM] * 2,
        out_specs=VMEM,
        scratch_shapes=[
            pltpu.VMEM((tokens * every, nope), F32),
            pltpu.VMEM((tokens * every, LANES), F32),
        ],
        compiler_params=params(8),
        cost_estimate=pl.CostEstimate(
            flops=2 * 10**8, bytes_accessed=3 * 10**6, transcendentals=0
        ),
        name="prompt_lift",
    )(in_vmem(prompt_query), in_vmem(key_up))


def attend(rate, group, heads, row_ref, key_ref, key_pos_ref, query_pos_ref, value_up_ref, put):
    tokens = query_pos_ref.shape[0]
    count = key_ref.shape[0]
    latent = value_up_ref.shape[1]
    visible = (key_pos_ref[:1, :] <= query_pos_ref[:, :1])[None]
    for first in range(heads.start, heads.stop, group):
        at = slice((first - heads.start) * tokens, (first - heads.start + group) * tokens)
        scores = dot_nt(row_ref[at, :], key_ref[...])
        scores = jnp.where(visible, scores.reshape(group, tokens, count), HIDDEN)
        scores = scores.reshape(group * tokens, count)
        weights = jnp.exp2((scores - jnp.max(scores, axis=1, keepdims=True)) * rate)
        total = jnp.sum(weights, axis=1, keepdims=True)
        mixed = dot(weights.astype(BF16), key_ref[:, :latent])
        mixed = (mixed / total).astype(BF16)
        for index in range(group):
            put(
                first + index,
                dot(
                    mixed[index * tokens : (index + 1) * tokens], value_up_ref[first + index]
                ).astype(BF16),
            )


def front_kernel(
    rate,
    group,
    heads,
    row_ref,
    key_ref,
    key_pos_ref,
    query_pos_ref,
    value_up_ref,
    weight_hbm,
    out_ref,
    weight_ref,
    sem,
):
    width = value_up_ref.shape[2]
    skipped = weight_hbm.shape[0] - weight_ref.shape[0]
    copy = pltpu.make_async_copy(weight_hbm.at[skipped:], weight_ref, sem)
    copy.start()

    def put(head, value):
        out_ref[:, head * width : (head + 1) * width] = value

    attend(
        rate, group, heads, row_ref, key_ref, key_pos_ref, query_pos_ref, value_up_ref, put
    )
    copy.wait()


def prompt_front(
    rate, group, heads, rows, keys, key_pos, query_pos, value_up, out_weight, late_rows
):
    tokens = query_pos.shape[0]
    shape = pltpu.VMEM
    return pl.pallas_call(
        functools.partial(front_kernel, rate, group, heads),
        out_shape=(
            shape((tokens, len(heads) * value_up.shape[2]), BF16),
            shape((late_rows, out_weight.shape[1]), BF16),
        ),
        in_specs=[VMEM] * 5 + [ANY],
        out_specs=[VMEM] * 2,
        scratch_shapes=[pltpu.SemaphoreType.DMA],
        compiler_params=params(16),
        cost_estimate=pl.CostEstimate(
            flops=8 * 10**8, bytes_accessed=6 * 10**6, transcendentals=3 * 10**5
        ),
        name="prompt_front",
    )(*(in_vmem(v) for v in (rows, keys, key_pos, query_pos, value_up)), in_hbm(out_weight))


def back_kernel(
    rate,
    group,
    heads,
    row_ref,
    key_ref,
    key_pos_ref,
    query_pos_ref,
    value_up_ref,
    front_ref,
    out_hbm,
    back_ref,
    sems,
):
    width = value_up_ref.shape[2]
    edge = heads.start * width
    copies = [pltpu.make_async_copy(front_ref, out_hbm.at[:, :edge], sems.at[0])]
    copies[0].start()

    def put(head, value):
        at = (head - heads.start) * width
        back_ref[:, at : at + width] = value
        if (head - heads.start + 1) % group == 0:
            start = at + width - group * width
            copies.append(
                pltpu.make_async_copy(
                    back_ref.at[:, start : at + width],
                    out_hbm.at[:, edge + start : edge + at + width],
                    sems.at[len(copies)],
                )
            )
            copies[-1].start()

    attend(
        rate, group, heads, row_ref, key_ref, key_pos_ref, query_pos_ref, value_up_ref, put
    )
    for copy in copies:
        copy.wait()


def prompt_back(rate, group, heads, rows, keys, key_pos, query_pos, value_up, front):
    tokens = query_pos.shape[0]
    width = value_up.shape[2]
    return pl.pallas_call(
        functools.partial(back_kernel, rate, group, heads),
        out_shape=jax.ShapeDtypeStruct((tokens, heads.stop * width), BF16),
        in_specs=[VMEM] * 6,
        out_specs=ANY,
        scratch_shapes=[
            pltpu.VMEM((tokens, len(heads) * width), BF16),
            pltpu.SemaphoreType.DMA((1 + len(heads) // group,)),
        ],
        compiler_params=params(16),
        cost_estimate=pl.CostEstimate(
            flops=8 * 10**8, bytes_accessed=6 * 10**6, transcendentals=3 * 10**5
        ),
        name="prompt_back",
    )(*(in_vmem(v) for v in (rows, keys, key_pos, query_pos, value_up, front)))


def per_device(
    prompt_query,
    prompt_latent,
    block_order,
    key_up,
    value_up,
    out_weight,
    step_query,
    cache_latent,
    step_latent,
    cache_length,
    block_dest,
):
    heads, width = prompt_query.shape[1:]
    rate = width ** (-0.5) * math.log2(math.e)
    context_size = lax.axis_size("ctx")
    steps = step_query.shape[0]
    head_size = lax.axis_size("head")
    role_size = lax.axis_size("role")
    contracted = out_weight.shape[0]
    early_rows = contracted // 2

    rounds = doublings(context_size)
    assert role_size == 2 and context_size >= 4
    far = swap(prompt_latent, "ctx", 2)
    (
        running,
        key_up,
        value_up,
        latent,
        prompt_query,
        early_weight,
        key_pos,
        query_pos,
    ) = step_part(
        rate,
        early_rows,
        block_order,
        cache_length,
        block_dest,
        step_query,
        key_up,
        jnp.swapaxes(cache_latent, 1, 2),
        prompt_latent,
        step_latent,
        value_up,
        prompt_query,
        out_weight,
    )
    group = 4 if heads % 8 == 0 else 1
    middle = heads // 2
    rows = prompt_lift(range(middle), prompt_query, key_up)
    more_rows = prompt_lift(range(middle, heads), prompt_query, key_up)
    for step in rounds:
        far_running = swap(running, "ctx", step)
        if step != rounds[-1]:
            running = merge_parts(rate, heads, running, far_running)
    tokens = latent.shape[0]
    mine = swap(move_rows(halves_kernel, tokens, latent, far), "ctx", 1)
    other = swap(mine, "role", 1)
    keys = move_rows(gather_kernel, 4 * tokens, latent, far, mine, other)
    for step in rounds[2:]:
        half = move_rows(half_kernel, keys.shape[0] // 2, keys)
        received = swap(half, "ctx", step)
        keys = move_rows(
            extend_kernel, 2 * keys.shape[0], keys, received, swap(received, "role", 1)
        )
    front, late_weight = prompt_front(
        rate,
        group,
        range(middle),
        rows,
        keys,
        key_pos,
        query_pos,
        value_up,
        out_weight,
        contracted - early_rows,
    )
    prompt_out = prompt_back(
        rate, group, range(middle, heads), more_rows, keys, key_pos, query_pos, value_up, front
    )
    keep, give = finish_steps(
        rate, heads, head_size * role_size, running, far_running, early_weight, late_weight
    )
    partial = swap(give, "role", 1)
    for step in reversed(doublings(head_size)):
        keep, give = fold_steps(step, keep, partial)
        partial = swap(give, "head", step)
    step_out = sum_steps(steps, keep, partial)
    return (prompt_out, step_out)


def solution(mesh):
    return jax.shard_map(
        per_device,
        mesh=mesh,
        in_specs=(
            P(("groups", "ctx"), ("head", "role"), None),
            P(("groups", "ctx"), None),
            P("groups"),
            P(("head", "role"), None, None),
            P(("head", "role"), None, None),
            P(("head", "role"), "ctx"),
            P(None, "groups", ("head", "role"), None),
            P("groups", "ctx", None),
            P(None, "groups", None),
            P("groups"),
            P("groups"),
        ),
        out_specs=(
            P(("groups", "ctx"), ("head", "role")),
            P(None, "groups", ("ctx", "head", "role")),
        ),
        check_vma=False,
    )
```

```python
import functools
import math

import jax
import jax.numpy as jnp
from jax import lax
from jax.experimental import pallas as pl
from jax.experimental.pallas import tpu as pltpu
from jax.sharding import PartitionSpec as P


BF16 = jnp.bfloat16
F32 = jnp.float32
LANES = 128
HIDDEN = -1e30
FLOOR = -1e29
TINY = 1e-30
MIB = 1 << 20

VMEM = pl.BlockSpec(memory_space=pltpu.VMEM)
ANY = pl.BlockSpec(memory_space=pl.ANY)
NT = (((1,), (1,)), ((), ()))


def dot(left, right):
    return jnp.dot(left, right, preferred_element_type=F32)


def dot_nt(left, right):
    return lax.dot_general(left, right, NT, preferred_element_type=F32)


def doublings(size):
    steps = []
    step = 1
    while step < size:
        steps.append(step)
        step *= 2
    assert step == size
    return steps


def swap(value, axis, step):
    size = lax.axis_size(axis)
    return lax.ppermute(value, axis, [(i, i ^ step) for i in range(size)])


def mark_kernel(out_ref):
    out_ref[...] = jnp.zeros_like(out_ref)


def mark():
    return pl.pallas_call(
        mark_kernel,
        out_shape=pltpu.VMEM((8, LANES), F32),
        out_specs=VMEM,
        compiler_params=params(1),
        cost_estimate=pl.CostEstimate(flops=8 * 10**9, bytes_accessed=10**4, transcendentals=0),
        name="mark",
    )()


def own_half_kernel(latent_hbm, out_ref, sem):
    half = out_ref.shape[0]
    start = pl.multiple_of(lax.axis_index("role") * half, half)
    copy = pltpu.make_async_copy(latent_hbm.at[pl.ds(start, half)], out_ref, sem)
    copy.start()
    copy.wait()


def own_half(latent):
    return pl.pallas_call(
        own_half_kernel,
        out_shape=pltpu.VMEM((latent.shape[0] // 2, latent.shape[1]), BF16),
        in_specs=[ANY],
        out_specs=VMEM,
        scratch_shapes=[pltpu.SemaphoreType.DMA],
        compiler_params=params(1),
        cost_estimate=pl.CostEstimate(flops=10**4, bytes_accessed=10**5, transcendentals=0),
        name="own_half",
    )(in_hbm(latent))


def in_hbm(value):
    return pltpu.with_memory_space_constraint(value, pltpu.HBM)


def in_vmem(value):
    return pltpu.with_memory_space_constraint(value, pltpu.VMEM)


def params(mib):
    return pltpu.CompilerParams(vmem_limit_bytes=mib * MIB)


def split_three(value):
    high = value.astype(BF16).astype(F32)
    rest = value - high
    middle = rest.astype(BF16).astype(F32)
    return high, middle, (rest - middle).astype(BF16).astype(F32)


def pick_piece(pieces, piece_ids):
    picked = pieces[-1]
    for index in reversed(range(len(pieces) - 1)):
        picked = jnp.where(piece_ids == index, pieces[index], picked)
    return picked


def step_kernel(
    rate,
    mark_ref,
    order_hbm,
    length_hbm,
    dest_hbm,
    query_ref,
    key_up_ref,
    cache_ref,
    latent_ref,
    fresh_ref,
    value_up_ref,
    prompt_hbm,
    out_ref,
    prompt_ref,
    key_pos_ref,
    query_pos_ref,
    order_ref,
    length_ref,
    dest_ref,
    nope_ref,
    row_ref,
    extra_ref,
    mixed_ref,
    sems,
):
    steps, requests, heads, width = query_ref.shape
    nope, latent = key_up_ref.shape[1:]
    span = cache_ref.shape[2]
    tokens = latent_ref.shape[0]
    pairs = steps * requests
    rows = pairs * heads
    block = steps * heads
    place = lax.axis_index("ctx")

    copies = []

    def fetch(source, target):
        copies.append(pltpu.make_async_copy(source, target, sems.at[len(copies)]))
        copies[-1].start()
        return copies[-1]

    scalar_copies = [
        fetch(length_hbm, length_ref),
        fetch(dest_hbm, dest_ref),
        fetch(order_hbm, order_ref),
    ]
    prompt_copy = fetch(prompt_hbm, prompt_ref)

    query = query_ref[...].astype(F32)
    query = jnp.concatenate(
        [query[:, request].reshape(block, width) for request in range(requests)], axis=0
    )
    nope_ref[...] = query[:, :nope]
    rope = query[:, nope:]
    for head in range(heads):
        part = nope_ref[pl.ds(head, pairs, stride=heads), :].astype(BF16)
        lifted = dot(part, key_up_ref[head]).astype(BF16).astype(F32)
        for lane in range(0, latent, LANES):
            row_ref[lane // LANES, pl.ds(head, pairs, stride=heads), :] = lifted[
                :, lane : lane + LANES
            ]
    row_parts = [row_ref[index] for index in range(latent // LANES)] + [rope]
    query_rows = jnp.concatenate(row_parts, axis=1).astype(BF16)

    extra_ref[:tokens, :] = latent_ref[...].astype(F32)
    for step in range(steps):
        extra_ref[tokens + step * requests : tokens + (step + 1) * requests, :] = fresh_ref[
            step
        ].astype(F32)
    extra = extra_ref[...].astype(BF16)
    more = dot_nt(query_rows, extra)
    for copy in scalar_copies:
        copy.wait()
    column = lax.broadcasted_iota(jnp.int32, more.shape, 1)
    row = lax.broadcasted_iota(jnp.int32, more.shape, 0)
    fresh_id = column - tokens
    seen = ((column < tokens) & (row // block == dest_ref[place])) | (
        (column >= tokens)
        & (fresh_id % requests == row // block)
        & (fresh_id // requests <= row // heads % steps)
        & (place == 0)
    )
    more = jnp.where(seen, more, HIDDEN)
    position = place * span + lax.broadcasted_iota(jnp.int32, (1, span), 1)
    scores = [
        jnp.where(
            position < length_ref[request],
            dot(query_rows[request * block : (request + 1) * block], cache_ref[request]),
            HIDDEN,
        )
        for request in range(requests)
    ]
    scores = jnp.concatenate(scores, axis=0)
    high = jnp.maximum(
        jnp.max(scores, axis=1, keepdims=True), jnp.max(more, axis=1, keepdims=True)
    )
    high = jnp.maximum(high, FLOOR)
    weights = jnp.exp2((scores - high) * rate)
    more = jnp.exp2((more - high) * rate)
    total = jnp.sum(weights, axis=1, keepdims=True) + jnp.sum(more, axis=1, keepdims=True)
    weights = weights.astype(BF16)
    mixed = jnp.concatenate(
        [
            dot_nt(weights[request * block : (request + 1) * block], cache_ref[request, :latent])
            for request in range(requests)
        ],
        axis=0,
    )
    mixed = mixed + dot(more.astype(BF16), extra[:, :latent])
    mixed = mixed * (1.0 / jnp.maximum(total, TINY))
    for lane in range(0, latent, LANES):
        mixed_ref[lane // LANES] = mixed[:, lane : lane + LANES]
    high = jnp.broadcast_to(high, (rows, LANES))
    total = jnp.broadcast_to(total, (rows, LANES))

    value_width = value_up_ref.shape[2]
    for head in range(heads):
        parts = [
            mixed_ref[index, pl.ds(head, pairs, stride=heads), :]
            for index in range(latent // LANES)
        ]
        part = jnp.concatenate(parts, axis=1).astype(BF16)
        out_ref[:, head * value_width : (head + 1) * value_width] = dot(
            part, value_up_ref[head]
        ).astype(BF16)
    lane = lax.broadcasted_iota(jnp.int32, (rows, LANES), 1)
    head_of_row = lax.broadcasted_iota(jnp.int32, (rows, LANES), 0) % heads
    pieces = split_three(high) + split_three(total)
    packed = pick_piece(pieces, lane // heads)
    packed = jnp.where((lane % heads == head_of_row) & (lane < 6 * heads), packed, 0.0)
    packed = jnp.sum(packed.reshape(pairs, heads, LANES), axis=1)
    out_ref[:, heads * value_width :] = packed.astype(BF16)

    key_id = lax.broadcasted_iota(jnp.int32, key_pos_ref.shape, 1)
    base = key_id
    for slot in range(key_pos_ref.shape[1] // tokens):
        move = (order_ref[place ^ slot] - slot) * tokens
        base = base + jnp.where(key_id // tokens == slot, move, 0)
    key_pos_ref[...] = base
    query_pos_ref[...] = order_ref[place] * tokens + lax.broadcasted_iota(
        jnp.int32, query_pos_ref.shape, 0
    )
    prompt_copy.wait()


def step_part(
    rate,
    block_order,
    cache_length,
    block_dest,
    step_query,
    key_up,
    cache,
    latent,
    fresh,
    value_up,
    prompt_query,
):
    steps, requests, heads, _ = step_query.shape
    nope, latent_width = key_up.shape[1:]
    full = cache.shape[1]
    tokens = latent.shape[0]
    pairs = steps * requests
    rows = pairs * heads
    shape = pltpu.VMEM
    return pl.pallas_call(
        functools.partial(step_kernel, rate),
        out_shape=(
            shape((pairs, heads * value_up.shape[2] + LANES), BF16),
            shape(prompt_query.shape, BF16),
            shape((8, tokens * lax.axis_size("ctx")), jnp.int32),
            shape((tokens, LANES), jnp.int32),
        ),
        in_specs=[VMEM] + [ANY] * 3 + [VMEM] * 6 + [ANY],
        out_specs=[VMEM] * 4,
        scratch_shapes=[
            pltpu.SMEM(block_order.shape, jnp.int32),
            pltpu.SMEM(cache_length.shape, jnp.int32),
            pltpu.SMEM(block_dest.shape, jnp.int32),
            pltpu.VMEM((rows, nope), F32),
            pltpu.VMEM((latent_width // LANES, rows, LANES), F32),
            pltpu.VMEM((tokens + pairs, full), F32),
            pltpu.VMEM((latent_width // LANES, rows, LANES), F32),
            pltpu.SemaphoreType.DMA((4,)),
        ],
        compiler_params=params(12),
        cost_estimate=pl.CostEstimate(flops=10**9, bytes_accessed=10**7, transcendentals=10**5),
        name="step_part",
    )(
        mark(),
        in_hbm(block_order),
        in_hbm(cache_length),
        in_hbm(block_dest),
        in_vmem(step_query),
        in_vmem(key_up),
        in_vmem(cache),
        in_vmem(latent),
        in_vmem(fresh),
        in_vmem(value_up),
        in_hbm(prompt_query),
    )


def read_stats(packed, heads):
    def piece(index):
        if index == 0:
            return packed
        return pltpu.roll(packed, LANES - index * heads, 1)

    return piece(0) + piece(1) + piece(2), piece(3) + piece(4) + piece(5)


def merge(rate, first_ref, second_ref, heads):
    split = first_ref.shape[1] - LANES
    value_width = split // heads
    high_a, total_a = read_stats(first_ref[:, split:].astype(F32), heads)
    high_b, total_b = read_stats(second_ref[:, split:].astype(F32), heads)
    high = jnp.maximum(high_a, high_b)
    share_a = total_a * jnp.exp2((high_a - high) * rate)
    share_b = total_b * jnp.exp2((high_b - high) * rate)
    total = share_a + share_b
    inverse = 1.0 / jnp.maximum(total, TINY)
    share_a = share_a * inverse
    share_b = share_b * inverse
    merged = []
    for head in range(heads):
        at = slice(head * value_width, (head + 1) * value_width)
        merged.append(
            (
                first_ref[:, at].astype(F32) * share_a[:, head : head + 1]
                + second_ref[:, at].astype(F32) * share_b[:, head : head + 1]
            ).astype(BF16)
        )
    return merged, high, total


def merge_kernel(rate, heads, first_ref, second_ref, out_ref):
    merged, high, total = merge(rate, first_ref, second_ref, heads)
    value_width = merged[0].shape[1]
    for head in range(heads):
        out_ref[:, head * value_width : (head + 1) * value_width] = merged[head]
    pieces = split_three(high) + split_three(total)
    lane = lax.broadcasted_iota(jnp.int32, high.shape, 1)
    moved = [p if i == 0 else pltpu.roll(p, i * heads, 1) for i, p in enumerate(pieces)]
    packed = jnp.where(lane < 6 * heads, pick_piece(moved, lane // heads), 0.0)
    out_ref[:, heads * value_width :] = packed.astype(BF16)


def merge_parts(rate, heads, first, second):
    return pl.pallas_call(
        functools.partial(merge_kernel, rate, heads),
        out_shape=pltpu.VMEM(first.shape, BF16),
        in_specs=[VMEM] * 2,
        out_specs=VMEM,
        compiler_params=params(2),
        cost_estimate=pl.CostEstimate(flops=10**5, bytes_accessed=2 * 10**5, transcendentals=10**4),
        name="merge_parts",
    )(in_vmem(first), in_vmem(second))


def join_kernel(first_ref, second_ref, out_ref):
    rows = first_ref.shape[0]
    out_ref[:rows, :] = first_ref[...]
    out_ref[rows:, :] = second_ref[...]


def gather_kernel(own_ref, mine_ref, other_ref, out_ref):
    tokens = own_ref.shape[0]
    half = tokens // 2
    out_ref[:tokens, :] = own_ref[...]
    for index, sources in enumerate(((mine_ref, other_ref), (other_ref, mine_ref))):

        @pl.when(lax.axis_index("role") == index)
        def _():
            for part, source in enumerate(sources):
                for place, slot in enumerate((2, 1, 3)):
                    at = slot * tokens + part * half
                    out_ref[at : at + half, :] = source[place * half : (place + 1) * half, :]


def half_kernel(keys_ref, out_ref):
    rows = out_ref.shape[0]
    for index in range(2):

        @pl.when(lax.axis_index("role") == index)
        def _():
            out_ref[...] = keys_ref[index * rows : (index + 1) * rows, :]


def extend_kernel(keys_ref, mine_ref, other_ref, out_ref):
    rows = keys_ref.shape[0]
    half = mine_ref.shape[0]
    out_ref[:rows, :] = keys_ref[...]
    for index, sources in enumerate(((mine_ref, other_ref), (other_ref, mine_ref))):

        @pl.when(lax.axis_index("role") == index)
        def _():
            out_ref[rows : rows + half, :] = sources[0][...]
            out_ref[rows + half :, :] = sources[1][...]


def move_rows(body, rows, *sources):
    return pl.pallas_call(
        body,
        out_shape=pltpu.VMEM((rows, sources[0].shape[1]), BF16),
        in_specs=[VMEM] * len(sources),
        out_specs=VMEM,
        compiler_params=params(1),
        cost_estimate=pl.CostEstimate(flops=10**4, bytes_accessed=4 * 10**5, transcendentals=0),
    )(*(in_vmem(source) for source in sources))


def finish_kernel(
    rate, heads, parts, first_ref, second_ref, weight_ref, keep_ref, give_ref
):
    merged, _, _ = merge(rate, first_ref, second_ref, heads)
    rows = jnp.concatenate(merged, axis=1)
    product = dot(rows, weight_ref[...])
    width = product.shape[1] // parts
    upper = lax.axis_index("role") == 1
    for index in range(parts // 2):
        low, high = (
            product[:, part * width : (part + 1) * width] for part in (2 * index, 2 * index + 1)
        )
        keep_ref[index] = jnp.where(upper, high, low)
        give_ref[index] = jnp.where(upper, low, high).astype(BF16)


def finish_steps(rate, heads, parts, first, second, weight):
    pairs = first.shape[0]
    shape = (parts // 2, pairs, weight.shape[1] // parts)
    return pl.pallas_call(
        functools.partial(finish_kernel, rate, heads, parts),
        out_shape=(pltpu.VMEM(shape, F32), pltpu.VMEM(shape, BF16)),
        in_specs=[VMEM] * 3,
        out_specs=[VMEM] * 2,
        compiler_params=params(4),
        cost_estimate=pl.CostEstimate(
            flops=5 * 10**8, bytes_accessed=8 * 10**6, transcendentals=10**4
        ),
        name="finish_steps",
    )(*(in_vmem(v) for v in (first, second, weight)))


def fold_kernel(step, keep_ref, received_ref, new_keep_ref, give_ref):
    share = keep_ref[...] + received_ref[...].astype(F32)
    middle = share.shape[0] // 2
    upper = lax.axis_index("head") & step != 0
    new_keep_ref[...] = jnp.where(upper, share[middle:], share[:middle])
    give_ref[...] = jnp.where(upper, share[:middle], share[middle:]).astype(BF16)


def fold_steps(step, keep, received):
    shape = (keep.shape[0] // 2, *keep.shape[1:])
    return pl.pallas_call(
        functools.partial(fold_kernel, step),
        out_shape=(pltpu.VMEM(shape, F32), pltpu.VMEM(shape, BF16)),
        in_specs=[VMEM] * 2,
        out_specs=[VMEM] * 2,
        compiler_params=params(1),
        cost_estimate=pl.CostEstimate(flops=10**5, bytes_accessed=10**5, transcendentals=0),
        name="fold_steps",
    )(in_vmem(keep), in_vmem(received))


def sum_kernel(keep_ref, received_ref, out_ref):
    share = keep_ref[0] + received_ref[0].astype(F32)
    steps, requests, _ = out_ref.shape
    for step in range(steps):
        rows = [share[at : at + 1] for at in range(step, steps * requests, steps)]
        out_ref[step] = jnp.concatenate(rows, axis=0).astype(BF16)


def sum_steps(steps, keep, received):
    pairs, width = keep.shape[1:]
    return pl.pallas_call(
        sum_kernel,
        out_shape=jax.ShapeDtypeStruct((steps, pairs // steps, width), BF16),
        in_specs=[VMEM] * 2,
        out_specs=VMEM,
        compiler_params=params(1),
        cost_estimate=pl.CostEstimate(flops=10**5, bytes_accessed=10**5, transcendentals=0),
        name="sum_steps",
    )(in_vmem(keep), in_vmem(received))


def lift_kernel(heads, query_ref, key_up_ref, row_ref, nope_ref, rope_ref):
    tokens, every, width = query_ref.shape
    nope, latent = key_up_ref.shape[1:]
    nope_ref[...] = query_ref[:, :, :nope].astype(F32).reshape(tokens * every, nope)
    rope_ref[:, : width - nope] = (
        query_ref[:, :, nope:].astype(F32).reshape(tokens * every, width - nope)
    )
    for index, head in enumerate(heads):
        at = slice(index * tokens, (index + 1) * tokens)
        part = nope_ref[pl.ds(head, tokens, stride=every), :].astype(BF16)
        row_ref[at, :latent] = dot(part, key_up_ref[head]).astype(BF16)
        rope = rope_ref[pl.ds(head, tokens, stride=every), :]
        row_ref[at, latent:] = rope[:, : width - nope].astype(BF16)


def prompt_lift(heads, prompt_query, key_up):
    tokens, every, width = prompt_query.shape
    nope, latent_width = key_up.shape[1:]
    return pl.pallas_call(
        functools.partial(lift_kernel, heads),
        out_shape=pltpu.VMEM((tokens * len(heads), latent_width + width - nope), BF16),
        in_specs=[VMEM] * 2,
        out_specs=VMEM,
        scratch_shapes=[
            pltpu.VMEM((tokens * every, nope), F32),
            pltpu.VMEM((tokens * every, LANES), F32),
        ],
        compiler_params=params(8),
        cost_estimate=pl.CostEstimate(
            flops=2 * 10**8, bytes_accessed=3 * 10**6, transcendentals=0
        ),
        name="prompt_lift",
    )(in_vmem(prompt_query), in_vmem(key_up))


def attend(
    rate, group, heads, row_ref, key_ref, key_pos_ref, query_pos_ref, value_up_ref, put
):
    tokens = query_pos_ref.shape[0]
    count = key_ref.shape[0]
    latent = value_up_ref.shape[1]
    visible = (key_pos_ref[:1, :] <= query_pos_ref[:, :1])[None]

    def score(first):
        base = first % (row_ref.shape[0] // tokens)
        at = slice(base * tokens, (base + group) * tokens)
        return dot_nt(row_ref[at, :], key_ref[...])

    firsts = list(range(heads.start, heads.stop, group))
    ahead = score(firsts[0])
    for first in firsts:
        scores = ahead
        if first != firsts[-1]:
            ahead = score(first + group)
        scores = jnp.where(visible, scores.reshape(group, tokens, count), HIDDEN)
        scores = scores.reshape(group * tokens, count)
        weights = jnp.exp2((scores - jnp.max(scores, axis=1, keepdims=True)) * rate)
        inverse = 1.0 / jnp.sum(weights, axis=1, keepdims=True)
        mixed = dot(weights.astype(BF16), key_ref[:, :latent]).astype(BF16)
        for index in range(group):
            part = slice(index * tokens, (index + 1) * tokens)
            value = dot(mixed[part], value_up_ref[first + index]) * inverse[part]
            put(first + index, value.astype(BF16))


def front_kernel(
    rate, group, heads, row_ref, key_ref, key_pos_ref, query_pos_ref, value_up_ref, out_ref
):
    width = value_up_ref.shape[2]

    def put(head, value):
        at = (head - heads.start) * width
        out_ref[:, at : at + width] = value

    attend(
        rate, group, heads, row_ref, key_ref, key_pos_ref, query_pos_ref, value_up_ref, put
    )


def prompt_front(rate, group, heads, rows, keys, key_pos, query_pos, value_up):
    tokens = query_pos.shape[0]
    return pl.pallas_call(
        functools.partial(front_kernel, rate, group, heads),
        out_shape=pltpu.VMEM((tokens, len(heads) * value_up.shape[2]), BF16),
        in_specs=[VMEM] * 5,
        out_specs=VMEM,
        compiler_params=params(16),
        cost_estimate=pl.CostEstimate(
            flops=4 * 10**8, bytes_accessed=3 * 10**6, transcendentals=3 * 10**5
        ),
        name="prompt_front",
    )(*(in_vmem(v) for v in (rows, keys, key_pos, query_pos, value_up)))


def back_kernel(
    rate,
    group,
    heads,
    row_ref,
    key_ref,
    key_pos_ref,
    query_pos_ref,
    value_up_ref,
    *refs,
):
    *front_refs, out_hbm, back_ref, sems = refs
    width = value_up_ref.shape[2]
    edge = 0
    copies = []
    for front_ref in front_refs:
        size = front_ref.shape[1]
        copies.append(
            pltpu.make_async_copy(
                front_ref, out_hbm.at[:, edge : edge + size], sems.at[len(copies)]
            )
        )
        copies[-1].start()
        edge += size
    assert edge == heads.start * width

    def put(head, value):
        at = (head - heads.start) * width
        back_ref[:, at : at + width] = value
        if (head - heads.start + 1) % group == 0:
            start = at + width - group * width
            copies.append(
                pltpu.make_async_copy(
                    back_ref.at[:, start : at + width],
                    out_hbm.at[:, edge + start : edge + at + width],
                    sems.at[len(copies)],
                )
            )
            copies[-1].start()

    attend(
        rate, group, heads, row_ref, key_ref, key_pos_ref, query_pos_ref, value_up_ref, put
    )
    for copy in copies:
        copy.wait()


def prompt_back(rate, group, heads, rows, keys, key_pos, query_pos, value_up, *fronts):
    tokens = query_pos.shape[0]
    width = value_up.shape[2]
    return pl.pallas_call(
        functools.partial(back_kernel, rate, group, heads),
        out_shape=jax.ShapeDtypeStruct((tokens, heads.stop * width), BF16),
        in_specs=[VMEM] * (5 + len(fronts)),
        out_specs=ANY,
        scratch_shapes=[
            pltpu.VMEM((tokens, len(heads) * width), BF16),
            pltpu.SemaphoreType.DMA((len(fronts) + len(heads) // group,)),
        ],
        compiler_params=params(16),
        cost_estimate=pl.CostEstimate(
            flops=8 * 10**8, bytes_accessed=6 * 10**6, transcendentals=3 * 10**5
        ),
        name="prompt_back",
    )(*(in_vmem(v) for v in (rows, keys, key_pos, query_pos, value_up, *fronts)))


def per_device(
    prompt_query,
    prompt_latent,
    block_order,
    key_up,
    value_up,
    out_weight,
    step_query,
    cache_latent,
    step_latent,
    cache_length,
    block_dest,
):
    heads, width = prompt_query.shape[1:]
    rate = width ** (-0.5) * math.log2(math.e)
    context_size = lax.axis_size("ctx")
    steps = step_query.shape[0]
    head_size = lax.axis_size("head")
    role_size = lax.axis_size("role")

    rounds = doublings(context_size)
    assert role_size == 2 and context_size >= 4
    half = own_half(prompt_latent)
    far = swap(half, "ctx", 2)
    (
        running,
        prompt_query,
        key_pos,
        query_pos,
    ) = step_part(
        rate,
        block_order,
        cache_length,
        block_dest,
        step_query,
        key_up,
        jnp.swapaxes(cache_latent, 1, 2),
        prompt_latent,
        step_latent,
        value_up,
        prompt_query,
    )
    group = 4 if heads % 16 == 0 else 2 if heads % 8 == 0 else 1
    middle = heads // 2
    rows = prompt_lift(range(middle), prompt_query, key_up)
    more_rows = prompt_lift(range(middle, heads), prompt_query, key_up)
    for step in rounds:
        far_running = swap(running, "ctx", step)
        if step != rounds[-1]:
            running = merge_parts(rate, heads, running, far_running)
    near = swap(move_rows(join_kernel, 2 * half.shape[0], half, far), "ctx", 1)
    mine = move_rows(join_kernel, 3 * half.shape[0], far, near)
    other = swap(mine, "role", 1)
    latent = prompt_latent
    keys = move_rows(gather_kernel, 4 * latent.shape[0], latent, mine, other)
    for step in rounds[2:]:
        sent = move_rows(half_kernel, keys.shape[0] // 2, keys)
        received = swap(sent, "ctx", step)
        keys = move_rows(
            extend_kernel, 2 * keys.shape[0], keys, received, swap(received, "role", 1)
        )
    first, second = range(middle // 2), range(middle // 2, middle)
    front_a = prompt_front(rate, group, first, rows, keys, key_pos, query_pos, value_up)
    front_b = prompt_front(rate, group, second, rows, keys, key_pos, query_pos, value_up)
    prompt_out = prompt_back(
        rate,
        group,
        range(middle, heads),
        more_rows,
        keys,
        key_pos,
        query_pos,
        value_up,
        front_a,
        front_b,
    )
    keep, give = finish_steps(
        rate, heads, head_size * role_size, running, far_running, out_weight
    )
    partial = swap(give, "role", 1)
    for step in reversed(doublings(head_size)):
        keep, give = fold_steps(step, keep, partial)
        partial = swap(give, "head", step)
    step_out = sum_steps(steps, keep, partial)
    return (prompt_out, step_out)


def solution(mesh):
    return jax.shard_map(
        per_device,
        mesh=mesh,
        in_specs=(
            P(("groups", "ctx"), ("head", "role"), None),
            P(("groups", "ctx"), None),
            P("groups"),
            P(("head", "role"), None, None),
            P(("head", "role"), None, None),
            P(("head", "role"), "ctx"),
            P(None, "groups", ("head", "role"), None),
            P("groups", "ctx", None),
            P(None, "groups", None),
            P("groups"),
            P("groups"),
        ),
        out_specs=(
            P(("groups", "ctx"), ("head", "role")),
            P(None, "groups", ("ctx", "head", "role")),
        ),
        check_vma=False,
    )
```

```python
import functools
import math

import jax
import jax.numpy as jnp
from jax import lax
from jax.experimental import pallas as pl
from jax.experimental.pallas import tpu as pltpu
from jax.sharding import PartitionSpec as P


BF16 = jnp.bfloat16
F32 = jnp.float32
LANES = 128
HIDDEN = -1e30
FLOOR = -1e29
TINY = 1e-30
MIB = 1 << 20

VMEM = pl.BlockSpec(memory_space=pltpu.VMEM)
ANY = pl.BlockSpec(memory_space=pl.ANY)
NT = (((1,), (1,)), ((), ()))


def dot(left, right):
    return jnp.dot(left, right, preferred_element_type=F32)


def dot_nt(left, right):
    return lax.dot_general(left, right, NT, preferred_element_type=F32)


def doublings(size):
    steps = []
    step = 1
    while step < size:
        steps.append(step)
        step *= 2
    assert step == size
    return steps


def swap(value, axis, step):
    size = lax.axis_size(axis)
    return lax.ppermute(value, axis, [(i, i ^ step) for i in range(size)])


def in_hbm(value):
    return pltpu.with_memory_space_constraint(value, pltpu.HBM)


def in_vmem(value):
    return pltpu.with_memory_space_constraint(value, pltpu.VMEM)


def params(mib):
    return pltpu.CompilerParams(vmem_limit_bytes=mib * MIB)


def split_three(value):
    high = value.astype(BF16).astype(F32)
    rest = value - high
    middle = rest.astype(BF16).astype(F32)
    return high, middle, (rest - middle).astype(BF16).astype(F32)


def pick_piece(pieces, piece_ids):
    picked = pieces[-1]
    for index in reversed(range(len(pieces) - 1)):
        picked = jnp.where(piece_ids == index, pieces[index], picked)
    return picked


def step_kernel(
    rate,
    order_hbm,
    length_hbm,
    dest_hbm,
    query_hbm,
    key_up_hbm,
    cache_hbm,
    latent_hbm,
    fresh_hbm,
    value_up_hbm,
    prompt_hbm,
    out_ref,
    key_up_ref,
    value_up_ref,
    latent_ref,
    half_ref,
    prompt_ref,
    key_pos_ref,
    query_pos_ref,
    order_ref,
    length_ref,
    dest_ref,
    query_ref,
    cache_ref,
    fresh_ref,
    nope_ref,
    row_ref,
    extra_ref,
    mixed_ref,
    sems,
):
    steps, requests, heads, width = query_ref.shape
    nope, latent = key_up_ref.shape[1:]
    span = cache_ref.shape[2]
    tokens = latent_ref.shape[0]
    pairs = steps * requests
    rows = pairs * heads
    block = steps * heads
    place = lax.axis_index("ctx")

    copies = []

    def fetch(source, target):
        copies.append(pltpu.make_async_copy(source, target, sems.at[len(copies)]))
        copies[-1].start()
        return copies[-1]

    query_copy = fetch(query_hbm, query_ref)
    quarter = heads // 4
    key_up_copies = [
        fetch(key_up_hbm.at[at : at + quarter], key_up_ref.at[at : at + quarter])
        for at in range(0, heads, quarter)
    ]
    latent_copy = fetch(latent_hbm, latent_ref)
    fresh_copy = fetch(fresh_hbm, fresh_ref)
    scalar_copies = [
        fetch(length_hbm, length_ref),
        fetch(dest_hbm, dest_ref),
        fetch(order_hbm, order_ref),
    ]
    cache_copy = fetch(cache_hbm, cache_ref)

    query_copy.wait()
    query = query_ref[...].astype(F32)
    query = jnp.concatenate(
        [query[:, request].reshape(block, width) for request in range(requests)], axis=0
    )
    nope_ref[...] = query[:, :nope]
    rope = query[:, nope:]
    for head in range(heads):
        if head % quarter == 0:
            key_up_copies[head // quarter].wait()
        part = nope_ref[pl.ds(head, pairs, stride=heads), :].astype(BF16)
        lifted = dot(part, key_up_ref[head]).astype(BF16).astype(F32)
        for lane in range(0, latent, LANES):
            row_ref[lane // LANES, pl.ds(head, pairs, stride=heads), :] = lifted[
                :, lane : lane + LANES
            ]
    value_up_copy = fetch(value_up_hbm, value_up_ref)
    prompt_copy = fetch(prompt_hbm, prompt_ref)
    row_parts = [row_ref[index] for index in range(latent // LANES)] + [rope]
    query_rows = jnp.concatenate(row_parts, axis=1).astype(BF16)

    latent_copy.wait()
    fresh_copy.wait()
    half = half_ref.shape[0]
    for index in range(2):

        @pl.when(lax.axis_index("role") == index)
        def _():
            half_ref[...] = latent_ref[index * half : (index + 1) * half, :]

    extra_ref[:tokens, :] = latent_ref[...].astype(F32)
    for step in range(steps):
        extra_ref[tokens + step * requests : tokens + (step + 1) * requests, :] = fresh_ref[
            step
        ].astype(F32)
    extra = extra_ref[...].astype(BF16)
    more = dot_nt(query_rows, extra)
    for copy in scalar_copies:
        copy.wait()
    column = lax.broadcasted_iota(jnp.int32, more.shape, 1)
    row = lax.broadcasted_iota(jnp.int32, more.shape, 0)
    fresh_id = column - tokens
    seen = ((column < tokens) & (row // block == dest_ref[place])) | (
        (column >= tokens)
        & (fresh_id % requests == row // block)
        & (fresh_id // requests <= row // heads % steps)
        & (place == 0)
    )
    more = jnp.where(seen, more, HIDDEN)
    position = place * span + lax.broadcasted_iota(jnp.int32, (1, span), 1)
    cache_copy.wait()
    scores = [
        jnp.where(
            position < length_ref[request],
            dot(query_rows[request * block : (request + 1) * block], cache_ref[request]),
            HIDDEN,
        )
        for request in range(requests)
    ]
    scores = jnp.concatenate(scores, axis=0)
    high = jnp.maximum(
        jnp.max(scores, axis=1, keepdims=True), jnp.max(more, axis=1, keepdims=True)
    )
    high = jnp.maximum(high, FLOOR)
    weights = jnp.exp2((scores - high) * rate)
    more = jnp.exp2((more - high) * rate)
    total = jnp.sum(weights, axis=1, keepdims=True) + jnp.sum(more, axis=1, keepdims=True)
    weights = weights.astype(BF16)
    mixed = jnp.concatenate(
        [
            dot_nt(weights[request * block : (request + 1) * block], cache_ref[request, :latent])
            for request in range(requests)
        ],
        axis=0,
    )
    mixed = mixed + dot(more.astype(BF16), extra[:, :latent])
    mixed = mixed * (1.0 / jnp.maximum(total, TINY))
    for lane in range(0, latent, LANES):
        mixed_ref[lane // LANES] = mixed[:, lane : lane + LANES]
    high = jnp.broadcast_to(high, (rows, LANES))
    total = jnp.broadcast_to(total, (rows, LANES))

    value_up_copy.wait()
    value_width = value_up_ref.shape[2]
    for head in range(heads):
        parts = [
            mixed_ref[index, pl.ds(head, pairs, stride=heads), :]
            for index in range(latent // LANES)
        ]
        part = jnp.concatenate(parts, axis=1).astype(BF16)
        out_ref[:, head * value_width : (head + 1) * value_width] = dot(
            part, value_up_ref[head]
        ).astype(BF16)
    lane = lax.broadcasted_iota(jnp.int32, (rows, LANES), 1)
    head_of_row = lax.broadcasted_iota(jnp.int32, (rows, LANES), 0) % heads
    pieces = split_three(high) + split_three(total)
    packed = pick_piece(pieces, lane // heads)
    packed = jnp.where((lane % heads == head_of_row) & (lane < 6 * heads), packed, 0.0)
    packed = jnp.sum(packed.reshape(pairs, heads, LANES), axis=1)
    out_ref[:, heads * value_width :] = packed.astype(BF16)

    key_id = lax.broadcasted_iota(jnp.int32, key_pos_ref.shape, 1)
    base = key_id
    for slot in range(key_pos_ref.shape[1] // tokens):
        move = (order_ref[place ^ slot] - slot) * tokens
        base = base + jnp.where(key_id // tokens == slot, move, 0)
    key_pos_ref[...] = base
    query_pos_ref[...] = order_ref[place] * tokens + lax.broadcasted_iota(
        jnp.int32, query_pos_ref.shape, 0
    )
    prompt_copy.wait()


def step_part(
    rate,
    block_order,
    cache_length,
    block_dest,
    step_query,
    key_up,
    cache,
    latent,
    fresh,
    value_up,
    prompt_query,
):
    steps, requests, heads, _ = step_query.shape
    nope, latent_width = key_up.shape[1:]
    full = cache.shape[1]
    tokens = latent.shape[0]
    pairs = steps * requests
    rows = pairs * heads
    shape = pltpu.VMEM
    return pl.pallas_call(
        functools.partial(step_kernel, rate),
        out_shape=(
            shape((pairs, heads * value_up.shape[2] + LANES), BF16),
            shape(key_up.shape, BF16),
            shape(value_up.shape, BF16),
            shape(latent.shape, BF16),
            shape((tokens // 2, full), BF16),
            shape(prompt_query.shape, BF16),
            shape((8, tokens * lax.axis_size("ctx")), jnp.int32),
            shape((tokens, LANES), jnp.int32),
        ),
        in_specs=[ANY] * 10,
        out_specs=[VMEM] * 8,
        scratch_shapes=[
            pltpu.SMEM(block_order.shape, jnp.int32),
            pltpu.SMEM(cache_length.shape, jnp.int32),
            pltpu.SMEM(block_dest.shape, jnp.int32),
            pltpu.VMEM(step_query.shape, BF16),
            pltpu.VMEM(cache.shape, BF16),
            pltpu.VMEM(fresh.shape, BF16),
            pltpu.VMEM((rows, nope), F32),
            pltpu.VMEM((latent_width // LANES, rows, LANES), F32),
            pltpu.VMEM((tokens + pairs, full), F32),
            pltpu.VMEM((latent_width // LANES, rows, LANES), F32),
            pltpu.SemaphoreType.DMA((13,)),
        ],
        compiler_params=params(16),
        cost_estimate=pl.CostEstimate(flops=10**9, bytes_accessed=10**7, transcendentals=10**5),
        name="step_part",
    )(
        *(
            in_hbm(value)
            for value in (
                block_order,
                cache_length,
                block_dest,
                step_query,
                key_up,
                cache,
                latent,
                fresh,
                value_up,
                prompt_query,
            )
        )
    )


def read_stats(packed, heads):
    def piece(index):
        if index == 0:
            return packed
        return pltpu.roll(packed, LANES - index * heads, 1)

    return piece(0) + piece(1) + piece(2), piece(3) + piece(4) + piece(5)


def merge(rate, first_ref, second_ref, heads):
    split = first_ref.shape[1] - LANES
    value_width = split // heads
    high_a, total_a = read_stats(first_ref[:, split:].astype(F32), heads)
    high_b, total_b = read_stats(second_ref[:, split:].astype(F32), heads)
    high = jnp.maximum(high_a, high_b)
    share_a = total_a * jnp.exp2((high_a - high) * rate)
    share_b = total_b * jnp.exp2((high_b - high) * rate)
    total = share_a + share_b
    inverse = 1.0 / jnp.maximum(total, TINY)
    share_a = share_a * inverse
    share_b = share_b * inverse
    merged = []
    for head in range(heads):
        at = slice(head * value_width, (head + 1) * value_width)
        merged.append(
            (
                first_ref[:, at].astype(F32) * share_a[:, head : head + 1]
                + second_ref[:, at].astype(F32) * share_b[:, head : head + 1]
            ).astype(BF16)
        )
    return merged, high, total


def merge_kernel(rate, heads, first_ref, second_ref, out_ref):
    merged, high, total = merge(rate, first_ref, second_ref, heads)
    value_width = merged[0].shape[1]
    for head in range(heads):
        out_ref[:, head * value_width : (head + 1) * value_width] = merged[head]
    pieces = split_three(high) + split_three(total)
    lane = lax.broadcasted_iota(jnp.int32, high.shape, 1)
    moved = [p if i == 0 else pltpu.roll(p, i * heads, 1) for i, p in enumerate(pieces)]
    packed = jnp.where(lane < 6 * heads, pick_piece(moved, lane // heads), 0.0)
    out_ref[:, heads * value_width :] = packed.astype(BF16)


def merge_parts(rate, heads, first, second):
    return pl.pallas_call(
        functools.partial(merge_kernel, rate, heads),
        out_shape=pltpu.VMEM(first.shape, BF16),
        in_specs=[VMEM] * 2,
        out_specs=VMEM,
        compiler_params=params(2),
        cost_estimate=pl.CostEstimate(
            flops=8 * 10**9, bytes_accessed=2 * 10**5, transcendentals=10**4
        ),
        name="merge_parts",
    )(in_vmem(first), in_vmem(second))


def join_kernel(first_ref, second_ref, out_ref):
    rows = first_ref.shape[0]
    out_ref[:rows, :] = first_ref[...]
    out_ref[rows:, :] = second_ref[...]


def gather_kernel(own_ref, mine_ref, other_ref, out_ref):
    tokens = own_ref.shape[0]
    half = tokens // 2
    out_ref[:tokens, :] = own_ref[...]
    for index, sources in enumerate(((mine_ref, other_ref), (other_ref, mine_ref))):

        @pl.when(lax.axis_index("role") == index)
        def _():
            for part, source in enumerate(sources):
                for place, slot in enumerate((2, 1, 3)):
                    at = slot * tokens + part * half
                    out_ref[at : at + half, :] = source[place * half : (place + 1) * half, :]


def half_kernel(keys_ref, out_ref):
    rows = out_ref.shape[0]
    for index in range(2):

        @pl.when(lax.axis_index("role") == index)
        def _():
            out_ref[...] = keys_ref[index * rows : (index + 1) * rows, :]


def extend_kernel(keys_ref, mine_ref, other_ref, out_ref):
    rows = keys_ref.shape[0]
    half = mine_ref.shape[0]
    out_ref[:rows, :] = keys_ref[...]
    for index, sources in enumerate(((mine_ref, other_ref), (other_ref, mine_ref))):

        @pl.when(lax.axis_index("role") == index)
        def _():
            out_ref[rows : rows + half, :] = sources[0][...]
            out_ref[rows + half :, :] = sources[1][...]


def move_rows(body, rows, *sources):
    return pl.pallas_call(
        body,
        out_shape=pltpu.VMEM((rows, sources[0].shape[1]), BF16),
        in_specs=[VMEM] * len(sources),
        out_specs=VMEM,
        compiler_params=params(1),
        cost_estimate=pl.CostEstimate(flops=10**4, bytes_accessed=4 * 10**5, transcendentals=0),
    )(*(in_vmem(source) for source in sources))


def finish_kernel(
    rate, heads, parts, first_ref, second_ref, weight_ref, keep_ref, give_ref
):
    merged, _, _ = merge(rate, first_ref, second_ref, heads)
    rows = jnp.concatenate(merged, axis=1)
    product = dot(rows, weight_ref[...])
    width = product.shape[1] // parts
    upper = lax.axis_index("role") == 1
    for index in range(parts // 2):
        low, high = (
            product[:, part * width : (part + 1) * width] for part in (2 * index, 2 * index + 1)
        )
        keep_ref[index] = jnp.where(upper, high, low)
        give_ref[index] = jnp.where(upper, low, high).astype(BF16)


def finish_steps(rate, heads, parts, first, second, weight):
    pairs = first.shape[0]
    shape = (parts // 2, pairs, weight.shape[1] // parts)
    return pl.pallas_call(
        functools.partial(finish_kernel, rate, heads, parts),
        out_shape=(pltpu.VMEM(shape, F32), pltpu.VMEM(shape, BF16)),
        in_specs=[VMEM] * 3,
        out_specs=[VMEM] * 2,
        compiler_params=params(4),
        cost_estimate=pl.CostEstimate(
            flops=5 * 10**8, bytes_accessed=8 * 10**6, transcendentals=10**4
        ),
        name="finish_steps",
    )(*(in_vmem(v) for v in (first, second, weight)))


def fold_kernel(step, keep_ref, received_ref, new_keep_ref, give_ref):
    share = keep_ref[...] + received_ref[...].astype(F32)
    middle = share.shape[0] // 2
    upper = lax.axis_index("head") & step != 0
    new_keep_ref[...] = jnp.where(upper, share[middle:], share[:middle])
    give_ref[...] = jnp.where(upper, share[:middle], share[middle:]).astype(BF16)


def fold_steps(step, keep, received):
    shape = (keep.shape[0] // 2, *keep.shape[1:])
    return pl.pallas_call(
        functools.partial(fold_kernel, step),
        out_shape=(pltpu.VMEM(shape, F32), pltpu.VMEM(shape, BF16)),
        in_specs=[VMEM] * 2,
        out_specs=[VMEM] * 2,
        compiler_params=params(1),
        cost_estimate=pl.CostEstimate(flops=10**5, bytes_accessed=10**5, transcendentals=0),
        name="fold_steps",
    )(in_vmem(keep), in_vmem(received))


def lift_kernel(query_ref, key_up_ref, row_ref, nope_ref, rope_ref):
    tokens, every, width = query_ref.shape
    nope, latent = key_up_ref.shape[1:]
    nope_ref[...] = query_ref[:, :, :nope].astype(F32).reshape(tokens * every, nope)
    rope_ref[:, : width - nope] = (
        query_ref[:, :, nope:].astype(F32).reshape(tokens * every, width - nope)
    )
    for head in range(every):
        at = slice(head * tokens, (head + 1) * tokens)
        part = nope_ref[pl.ds(head, tokens, stride=every), :].astype(BF16)
        row_ref[at, :latent] = dot(part, key_up_ref[head]).astype(BF16)
        rope = rope_ref[pl.ds(head, tokens, stride=every), :]
        row_ref[at, latent:] = rope[:, : width - nope].astype(BF16)


def prompt_lift(prompt_query, key_up):
    tokens, every, width = prompt_query.shape
    nope, latent_width = key_up.shape[1:]
    return pl.pallas_call(
        lift_kernel,
        out_shape=pltpu.VMEM((tokens * every, latent_width + width - nope), BF16),
        in_specs=[VMEM] * 2,
        out_specs=VMEM,
        scratch_shapes=[
            pltpu.VMEM((tokens * every, nope), F32),
            pltpu.VMEM((tokens * every, LANES), F32),
        ],
        compiler_params=params(8),
        cost_estimate=pl.CostEstimate(
            flops=8 * 10**8, bytes_accessed=3 * 10**6, transcendentals=0
        ),
        name="prompt_lift",
    )(in_vmem(prompt_query), in_vmem(key_up))


def attend(
    rate, group, heads, row_ref, key_ref, key_pos_ref, query_pos_ref, value_up_ref, put
):
    tokens = query_pos_ref.shape[0]
    count = key_ref.shape[0]
    latent = value_up_ref.shape[1]
    visible = (key_pos_ref[:1, :] <= query_pos_ref[:, :1])[None]

    def score(first):
        at = slice(first * tokens, (first + group) * tokens)
        return dot_nt(row_ref[at, :], key_ref[...])

    firsts = list(range(heads.start, heads.stop, group))
    ahead = score(firsts[0])
    for first in firsts:
        scores = ahead
        if first != firsts[-1]:
            ahead = score(first + group)
        scores = jnp.where(visible, scores.reshape(group, tokens, count), HIDDEN)
        scores = scores.reshape(group * tokens, count)
        weights = jnp.exp2((scores - jnp.max(scores, axis=1, keepdims=True)) * rate)
        inverse = 1.0 / jnp.sum(weights, axis=1, keepdims=True)
        mixed = dot(weights.astype(BF16), key_ref[:, :latent]).astype(BF16)
        for index in range(group):
            part = slice(index * tokens, (index + 1) * tokens)
            value = dot(mixed[part], value_up_ref[first + index]) * inverse[part]
            put(first + index, value.astype(BF16))


def front_kernel(
    rate, group, heads, row_ref, key_ref, key_pos_ref, query_pos_ref, value_up_ref, out_ref
):
    width = value_up_ref.shape[2]

    def put(head, value):
        at = (head - heads.start) * width
        out_ref[:, at : at + width] = value

    attend(
        rate, group, heads, row_ref, key_ref, key_pos_ref, query_pos_ref, value_up_ref, put
    )


def prompt_front(rate, group, heads, rows, keys, key_pos, query_pos, value_up):
    tokens = query_pos.shape[0]
    return pl.pallas_call(
        functools.partial(front_kernel, rate, group, heads),
        out_shape=pltpu.VMEM((tokens, len(heads) * value_up.shape[2]), BF16),
        in_specs=[VMEM] * 5,
        out_specs=VMEM,
        compiler_params=params(16),
        cost_estimate=pl.CostEstimate(
            flops=4 * 10**8, bytes_accessed=3 * 10**6, transcendentals=3 * 10**5
        ),
        name="prompt_front",
    )(*(in_vmem(v) for v in (rows, keys, key_pos, query_pos, value_up)))


def back_kernel(
    rate,
    group,
    heads,
    row_ref,
    key_ref,
    key_pos_ref,
    query_pos_ref,
    value_up_ref,
    front_ref,
    keep_ref,
    received_ref,
    out_hbm,
    steps_hbm,
    back_ref,
    steps_ref,
    sems,
):
    width = value_up_ref.shape[2]
    edge = heads.start * width
    copies = []

    def send(source, target):
        copies.append(pltpu.make_async_copy(source, target, sems.at[len(copies)]))
        copies[-1].start()

    send(front_ref, out_hbm.at[:, :edge])
    share = keep_ref[0] + received_ref[0].astype(F32)
    steps, requests, _ = steps_ref.shape
    for step in range(steps):
        rows = [share[at : at + 1] for at in range(step, steps * requests, steps)]
        steps_ref[step] = jnp.concatenate(rows, axis=0).astype(BF16)
    send(steps_ref, steps_hbm)

    def put(head, value):
        at = (head - heads.start) * width
        back_ref[:, at : at + width] = value
        if (head - heads.start + 1) % group == 0:
            start = at + width - group * width
            send(
                back_ref.at[:, start : at + width],
                out_hbm.at[:, edge + start : edge + at + width],
            )

    attend(
        rate, group, heads, row_ref, key_ref, key_pos_ref, query_pos_ref, value_up_ref, put
    )
    for copy in copies:
        copy.wait()


def prompt_back(
    rate, group, heads, steps, rows, keys, key_pos, query_pos, value_up, front, keep, received
):
    tokens = query_pos.shape[0]
    width = value_up.shape[2]
    pairs, columns = keep.shape[1:]
    step_shape = (steps, pairs // steps, columns)
    return pl.pallas_call(
        functools.partial(back_kernel, rate, group, heads),
        out_shape=(
            jax.ShapeDtypeStruct((tokens, heads.stop * width), BF16),
            jax.ShapeDtypeStruct(step_shape, BF16),
        ),
        in_specs=[VMEM] * 8,
        out_specs=[ANY] * 2,
        scratch_shapes=[
            pltpu.VMEM((tokens, len(heads) * width), BF16),
            pltpu.VMEM(step_shape, BF16),
            pltpu.SemaphoreType.DMA((2 + len(heads) // group,)),
        ],
        compiler_params=params(16),
        cost_estimate=pl.CostEstimate(
            flops=8 * 10**8, bytes_accessed=6 * 10**6, transcendentals=3 * 10**5
        ),
        name="prompt_back",
    )(
        *(
            in_vmem(v)
            for v in (rows, keys, key_pos, query_pos, value_up, front, keep, received)
        )
    )


def per_device(
    prompt_query,
    prompt_latent,
    block_order,
    key_up,
    value_up,
    out_weight,
    step_query,
    cache_latent,
    step_latent,
    cache_length,
    block_dest,
):
    heads, width = prompt_query.shape[1:]
    rate = width ** (-0.5) * math.log2(math.e)
    context_size = lax.axis_size("ctx")
    steps = step_query.shape[0]
    head_size = lax.axis_size("head")
    role_size = lax.axis_size("role")

    rounds = doublings(context_size)
    assert role_size == 2 and context_size >= 4
    (
        running,
        key_up,
        value_up,
        latent,
        half,
        prompt_query,
        key_pos,
        query_pos,
    ) = step_part(
        rate,
        block_order,
        cache_length,
        block_dest,
        step_query,
        key_up,
        jnp.swapaxes(cache_latent, 1, 2),
        prompt_latent,
        step_latent,
        value_up,
        prompt_query,
    )
    group = 4 if heads % 16 == 0 else 2 if heads % 8 == 0 else 1
    edge = heads - heads // 4
    rows = prompt_lift(prompt_query, key_up)
    for step in rounds:
        far_running = swap(running, "ctx", step)
        if step != rounds[-1]:
            running = merge_parts(rate, heads, running, far_running)
    far = swap(half, "ctx", 2)
    near = swap(move_rows(join_kernel, 2 * half.shape[0], half, far), "ctx", 1)
    mine = move_rows(join_kernel, 3 * half.shape[0], far, near)
    other = swap(mine, "role", 1)
    keys = move_rows(gather_kernel, 4 * latent.shape[0], latent, mine, other)
    for step in rounds[2:]:
        sent = move_rows(half_kernel, keys.shape[0] // 2, keys)
        received = swap(sent, "ctx", step)
        keys = move_rows(
            extend_kernel, 2 * keys.shape[0], keys, received, swap(received, "role", 1)
        )
    front = prompt_front(rate, group, range(edge), rows, keys, key_pos, query_pos, value_up)
    keep, give = finish_steps(
        rate, heads, head_size * role_size, running, far_running, out_weight
    )
    partial = swap(give, "role", 1)
    for step in reversed(doublings(head_size)):
        keep, give = fold_steps(step, keep, partial)
        partial = swap(give, "head", step)
    return prompt_back(
        rate,
        group,
        range(edge, heads),
        steps,
        rows,
        keys,
        key_pos,
        query_pos,
        value_up,
        front,
        keep,
        partial,
    )


def solution(mesh):
    return jax.shard_map(
        per_device,
        mesh=mesh,
        in_specs=(
            P(("groups", "ctx"), ("head", "role"), None),
            P(("groups", "ctx"), None),
            P("groups"),
            P(("head", "role"), None, None),
            P(("head", "role"), None, None),
            P(("head", "role"), "ctx"),
            P(None, "groups", ("head", "role"), None),
            P("groups", "ctx", None),
            P(None, "groups", None),
            P("groups"),
            P("groups"),
        ),
        out_specs=(
            P(("groups", "ctx"), ("head", "role")),
            P(None, "groups", ("ctx", "head", "role")),
        ),
        check_vma=False,
    )
```

```python
import functools
import math

import jax
import jax.numpy as jnp
from jax import lax
from jax.experimental import pallas as pl
from jax.experimental.pallas import tpu as pltpu
from jax.sharding import PartitionSpec as P


BF16 = jnp.bfloat16
F32 = jnp.float32
LANES = 128
HIDDEN = -1e30
FLOOR = -1e29
TINY = 1e-30
MIB = 1 << 20

VMEM = pl.BlockSpec(memory_space=pltpu.VMEM)
ANY = pl.BlockSpec(memory_space=pl.ANY)
NT = (((1,), (1,)), ((), ()))


def dot(left, right):
    return jnp.dot(left, right, preferred_element_type=F32)


def dot_nt(left, right):
    return lax.dot_general(left, right, NT, preferred_element_type=F32)


def doublings(size):
    steps = []
    step = 1
    while step < size:
        steps.append(step)
        step *= 2
    assert step == size
    return steps


def swap(value, axis, step):
    size = lax.axis_size(axis)
    return lax.ppermute(value, axis, [(i, i ^ step) for i in range(size)])


def in_hbm(value):
    return pltpu.with_memory_space_constraint(value, pltpu.HBM)


def in_vmem(value):
    return pltpu.with_memory_space_constraint(value, pltpu.VMEM)


def params(mib):
    return pltpu.CompilerParams(vmem_limit_bytes=mib * MIB)


def split_three(value):
    high = value.astype(BF16).astype(F32)
    rest = value - high
    middle = rest.astype(BF16).astype(F32)
    return high, middle, (rest - middle).astype(BF16).astype(F32)


def pick_piece(pieces, piece_ids):
    picked = pieces[-1]
    for index in reversed(range(len(pieces) - 1)):
        picked = jnp.where(piece_ids == index, pieces[index], picked)
    return picked


def step_kernel(
    rate,
    order_hbm,
    length_hbm,
    dest_hbm,
    query_hbm,
    key_up_hbm,
    cache_hbm,
    latent_hbm,
    fresh_hbm,
    value_up_hbm,
    prompt_hbm,
    out_ref,
    key_up_ref,
    value_up_ref,
    latent_ref,
    half_ref,
    prompt_ref,
    key_pos_ref,
    query_pos_ref,
    order_ref,
    length_ref,
    dest_ref,
    query_ref,
    cache_ref,
    fresh_ref,
    nope_ref,
    row_ref,
    extra_ref,
    mixed_ref,
    sems,
):
    steps, requests, heads, width = query_ref.shape
    nope, latent = key_up_ref.shape[1:]
    span = cache_ref.shape[2]
    tokens = latent_ref.shape[0]
    pairs = steps * requests
    rows = pairs * heads
    block = steps * heads
    place = lax.axis_index("ctx")

    copies = []

    def fetch(source, target):
        copies.append(pltpu.make_async_copy(source, target, sems.at[len(copies)]))
        copies[-1].start()
        return copies[-1]

    query_copy = fetch(query_hbm, query_ref)
    chunk = heads // 2
    key_up_copies = [
        fetch(key_up_hbm.at[at : at + chunk], key_up_ref.at[at : at + chunk])
        for at in range(0, heads, chunk)
    ]
    latent_copy = fetch(latent_hbm, latent_ref)
    fresh_copy = fetch(fresh_hbm, fresh_ref)
    scalar_copies = [
        fetch(length_hbm, length_ref),
        fetch(dest_hbm, dest_ref),
        fetch(order_hbm, order_ref),
    ]
    cache_copy = fetch(cache_hbm, cache_ref)

    query_copy.wait()
    query = query_ref[...].astype(F32)
    query = jnp.concatenate(
        [query[:, request].reshape(block, width) for request in range(requests)], axis=0
    )
    nope_ref[...] = query[:, :nope]
    rope = query[:, nope:]
    for head in range(heads):
        if head % chunk == 0:
            key_up_copies[head // chunk].wait()
        part = nope_ref[pl.ds(head, pairs, stride=heads), :].astype(BF16)
        lifted = dot(part, key_up_ref[head]).astype(BF16).astype(F32)
        for lane in range(0, latent, LANES):
            row_ref[lane // LANES, pl.ds(head, pairs, stride=heads), :] = lifted[
                :, lane : lane + LANES
            ]
    value_up_copy = fetch(value_up_hbm, value_up_ref)
    prompt_copy = fetch(prompt_hbm, prompt_ref)
    row_parts = [row_ref[index] for index in range(latent // LANES)] + [rope]
    query_rows = jnp.concatenate(row_parts, axis=1).astype(BF16)

    latent_copy.wait()
    fresh_copy.wait()
    half = half_ref.shape[0]
    for index in range(2):

        @pl.when(lax.axis_index("role") == index)
        def _():
            half_ref[...] = latent_ref[index * half : (index + 1) * half, :]

    extra_ref[:tokens, :] = latent_ref[...].astype(F32)
    for step in range(steps):
        extra_ref[tokens + step * requests : tokens + (step + 1) * requests, :] = fresh_ref[
            step
        ].astype(F32)
    extra = extra_ref[...].astype(BF16)
    more = dot_nt(query_rows, extra)
    for copy in scalar_copies:
        copy.wait()
    column = lax.broadcasted_iota(jnp.int32, more.shape, 1)
    row = lax.broadcasted_iota(jnp.int32, more.shape, 0)
    fresh_id = column - tokens
    seen = ((column < tokens) & (row // block == dest_ref[place])) | (
        (column >= tokens)
        & (fresh_id % requests == row // block)
        & (fresh_id // requests <= row // heads % steps)
        & (place == 0)
    )
    more = jnp.where(seen, more, HIDDEN)
    position = place * span + lax.broadcasted_iota(jnp.int32, (1, span), 1)
    cache_copy.wait()
    scores = [
        jnp.where(
            position < length_ref[request],
            dot(query_rows[request * block : (request + 1) * block], cache_ref[request]),
            HIDDEN,
        )
        for request in range(requests)
    ]
    scores = jnp.concatenate(scores, axis=0)
    high = jnp.maximum(
        jnp.max(scores, axis=1, keepdims=True), jnp.max(more, axis=1, keepdims=True)
    )
    high = jnp.maximum(high, FLOOR)
    weights = jnp.exp2((scores - high) * rate)
    more = jnp.exp2((more - high) * rate)
    total = jnp.sum(weights, axis=1, keepdims=True) + jnp.sum(more, axis=1, keepdims=True)
    weights = weights.astype(BF16)
    mixed = jnp.concatenate(
        [
            dot_nt(weights[request * block : (request + 1) * block], cache_ref[request, :latent])
            for request in range(requests)
        ],
        axis=0,
    )
    mixed = mixed + dot(more.astype(BF16), extra[:, :latent])
    mixed = mixed * (1.0 / jnp.maximum(total, TINY))
    for lane in range(0, latent, LANES):
        mixed_ref[lane // LANES] = mixed[:, lane : lane + LANES]
    high = jnp.broadcast_to(high, (rows, LANES))
    total = jnp.broadcast_to(total, (rows, LANES))

    value_up_copy.wait()
    value_width = value_up_ref.shape[2]
    for head in range(heads):
        parts = [
            mixed_ref[index, pl.ds(head, pairs, stride=heads), :]
            for index in range(latent // LANES)
        ]
        part = jnp.concatenate(parts, axis=1).astype(BF16)
        out_ref[:, head * value_width : (head + 1) * value_width] = dot(
            part, value_up_ref[head]
        ).astype(BF16)
    lane = lax.broadcasted_iota(jnp.int32, (rows, LANES), 1)
    head_of_row = lax.broadcasted_iota(jnp.int32, (rows, LANES), 0) % heads
    pieces = split_three(high) + split_three(total)
    packed = pick_piece(pieces, lane // heads)
    packed = jnp.where((lane % heads == head_of_row) & (lane < 6 * heads), packed, 0.0)
    packed = jnp.sum(packed.reshape(pairs, heads, LANES), axis=1)
    out_ref[:, heads * value_width :] = packed.astype(BF16)

    key_id = lax.broadcasted_iota(jnp.int32, key_pos_ref.shape, 1)
    base = key_id
    for slot in range(key_pos_ref.shape[1] // tokens):
        move = (order_ref[place ^ slot] - slot) * tokens
        base = base + jnp.where(key_id // tokens == slot, move, 0)
    key_pos_ref[...] = base
    query_pos_ref[...] = order_ref[place] * tokens + lax.broadcasted_iota(
        jnp.int32, query_pos_ref.shape, 0
    )
    prompt_copy.wait()


def step_part(
    rate,
    block_order,
    cache_length,
    block_dest,
    step_query,
    key_up,
    cache,
    latent,
    fresh,
    value_up,
    prompt_query,
):
    steps, requests, heads, _ = step_query.shape
    nope, latent_width = key_up.shape[1:]
    full = cache.shape[1]
    tokens = latent.shape[0]
    pairs = steps * requests
    rows = pairs * heads
    shape = pltpu.VMEM
    return pl.pallas_call(
        functools.partial(step_kernel, rate),
        out_shape=(
            shape((pairs, heads * value_up.shape[2] + LANES), BF16),
            shape(key_up.shape, BF16),
            shape(value_up.shape, BF16),
            shape(latent.shape, BF16),
            shape((tokens // 2, full), BF16),
            shape(prompt_query.shape, BF16),
            shape((8, tokens * lax.axis_size("ctx")), jnp.int32),
            shape((tokens, LANES), jnp.int32),
        ),
        in_specs=[ANY] * 10,
        out_specs=[VMEM] * 8,
        scratch_shapes=[
            pltpu.SMEM(block_order.shape, jnp.int32),
            pltpu.SMEM(cache_length.shape, jnp.int32),
            pltpu.SMEM(block_dest.shape, jnp.int32),
            pltpu.VMEM(step_query.shape, BF16),
            pltpu.VMEM(cache.shape, BF16),
            pltpu.VMEM(fresh.shape, BF16),
            pltpu.VMEM((rows, nope), F32),
            pltpu.VMEM((latent_width // LANES, rows, LANES), F32),
            pltpu.VMEM((tokens + pairs, full), F32),
            pltpu.VMEM((latent_width // LANES, rows, LANES), F32),
            pltpu.SemaphoreType.DMA((11,)),
        ],
        compiler_params=params(16),
        cost_estimate=pl.CostEstimate(flops=10**9, bytes_accessed=10**7, transcendentals=10**5),
        name="step_part",
    )(
        *(
            in_hbm(value)
            for value in (
                block_order,
                cache_length,
                block_dest,
                step_query,
                key_up,
                cache,
                latent,
                fresh,
                value_up,
                prompt_query,
            )
        )
    )


def read_stats(packed, heads):
    def piece(index):
        if index == 0:
            return packed
        return pltpu.roll(packed, LANES - index * heads, 1)

    return piece(0) + piece(1) + piece(2), piece(3) + piece(4) + piece(5)


def merge(rate, first_ref, second_ref, heads):
    split = first_ref.shape[1] - LANES
    value_width = split // heads
    high_a, total_a = read_stats(first_ref[:, split:].astype(F32), heads)
    high_b, total_b = read_stats(second_ref[:, split:].astype(F32), heads)
    high = jnp.maximum(high_a, high_b)
    share_a = total_a * jnp.exp2((high_a - high) * rate)
    share_b = total_b * jnp.exp2((high_b - high) * rate)
    total = share_a + share_b
    inverse = 1.0 / jnp.maximum(total, TINY)
    share_a = share_a * inverse
    share_b = share_b * inverse
    merged = []
    for head in range(heads):
        at = slice(head * value_width, (head + 1) * value_width)
        merged.append(
            (
                first_ref[:, at].astype(F32) * share_a[:, head : head + 1]
                + second_ref[:, at].astype(F32) * share_b[:, head : head + 1]
            ).astype(BF16)
        )
    return merged, high, total


def merge_kernel(rate, heads, first_ref, second_ref, out_ref):
    merged, high, total = merge(rate, first_ref, second_ref, heads)
    value_width = merged[0].shape[1]
    for head in range(heads):
        out_ref[:, head * value_width : (head + 1) * value_width] = merged[head]
    pieces = split_three(high) + split_three(total)
    lane = lax.broadcasted_iota(jnp.int32, high.shape, 1)
    moved = [p if i == 0 else pltpu.roll(p, i * heads, 1) for i, p in enumerate(pieces)]
    packed = jnp.where(lane < 6 * heads, pick_piece(moved, lane // heads), 0.0)
    out_ref[:, heads * value_width :] = packed.astype(BF16)


def merge_parts(rate, heads, first, second):
    return pl.pallas_call(
        functools.partial(merge_kernel, rate, heads),
        out_shape=pltpu.VMEM(first.shape, BF16),
        in_specs=[VMEM] * 2,
        out_specs=VMEM,
        compiler_params=params(2),
        cost_estimate=pl.CostEstimate(
            flops=8 * 10**9, bytes_accessed=2 * 10**5, transcendentals=10**4
        ),
        name="merge_parts",
    )(in_vmem(first), in_vmem(second))


def join_kernel(first_ref, second_ref, out_ref):
    rows = first_ref.shape[0]
    out_ref[:rows, :] = first_ref[...]
    out_ref[rows:, :] = second_ref[...]


def gather_kernel(own_ref, mine_ref, other_ref, out_ref):
    tokens = own_ref.shape[0]
    half = tokens // 2
    out_ref[:tokens, :] = own_ref[...]
    for index, sources in enumerate(((mine_ref, other_ref), (other_ref, mine_ref))):

        @pl.when(lax.axis_index("role") == index)
        def _():
            for part, source in enumerate(sources):
                for place, slot in enumerate((2, 1, 3)):
                    at = slot * tokens + part * half
                    out_ref[at : at + half, :] = source[place * half : (place + 1) * half, :]


def half_kernel(keys_ref, out_ref):
    rows = out_ref.shape[0]
    for index in range(2):

        @pl.when(lax.axis_index("role") == index)
        def _():
            out_ref[...] = keys_ref[index * rows : (index + 1) * rows, :]


def extend_kernel(keys_ref, mine_ref, other_ref, out_ref):
    rows = keys_ref.shape[0]
    half = mine_ref.shape[0]
    out_ref[:rows, :] = keys_ref[...]
    for index, sources in enumerate(((mine_ref, other_ref), (other_ref, mine_ref))):

        @pl.when(lax.axis_index("role") == index)
        def _():
            out_ref[rows : rows + half, :] = sources[0][...]
            out_ref[rows + half :, :] = sources[1][...]


def move_rows(body, rows, *sources):
    return pl.pallas_call(
        body,
        out_shape=pltpu.VMEM((rows, sources[0].shape[1]), BF16),
        in_specs=[VMEM] * len(sources),
        out_specs=VMEM,
        compiler_params=params(1),
        cost_estimate=pl.CostEstimate(flops=10**4, bytes_accessed=4 * 10**5, transcendentals=0),
    )(*(in_vmem(source) for source in sources))


def finish_kernel(
    rate, heads, parts, first_ref, second_ref, weight_ref, keep_ref, give_ref
):
    merged, _, _ = merge(rate, first_ref, second_ref, heads)
    chunk = heads // 2
    size = chunk * merged[0].shape[1]
    product = 0.0
    for index in range(2):
        rows = jnp.concatenate(merged[index * chunk : (index + 1) * chunk], axis=1)
        product = product + dot(rows, weight_ref[index * size : (index + 1) * size, :])
    width = product.shape[1] // parts
    upper = lax.axis_index("role") == 1
    for index in range(parts // 2):
        low, high = (
            product[:, part * width : (part + 1) * width] for part in (2 * index, 2 * index + 1)
        )
        keep_ref[index] = jnp.where(upper, high, low)
        give_ref[index] = jnp.where(upper, low, high).astype(BF16)


def finish_steps(rate, heads, parts, first, second, weight):
    pairs = first.shape[0]
    shape = (parts // 2, pairs, weight.shape[1] // parts)
    return pl.pallas_call(
        functools.partial(finish_kernel, rate, heads, parts),
        out_shape=(pltpu.VMEM(shape, F32), pltpu.VMEM(shape, BF16)),
        in_specs=[VMEM] * 3,
        out_specs=[VMEM] * 2,
        compiler_params=params(4),
        cost_estimate=pl.CostEstimate(
            flops=5 * 10**8, bytes_accessed=8 * 10**6, transcendentals=10**4
        ),
        name="finish_steps",
    )(*(in_vmem(v) for v in (first, second, weight)))


def fold_kernel(step, keep_ref, received_ref, new_keep_ref, give_ref):
    share = keep_ref[...] + received_ref[...].astype(F32)
    middle = share.shape[0] // 2
    upper = lax.axis_index("head") & step != 0
    new_keep_ref[...] = jnp.where(upper, share[middle:], share[:middle])
    give_ref[...] = jnp.where(upper, share[:middle], share[middle:]).astype(BF16)


def fold_steps(step, keep, received):
    shape = (keep.shape[0] // 2, *keep.shape[1:])
    return pl.pallas_call(
        functools.partial(fold_kernel, step),
        out_shape=(pltpu.VMEM(shape, F32), pltpu.VMEM(shape, BF16)),
        in_specs=[VMEM] * 2,
        out_specs=[VMEM] * 2,
        compiler_params=params(1),
        cost_estimate=pl.CostEstimate(flops=10**5, bytes_accessed=10**5, transcendentals=0),
        name="fold_steps",
    )(in_vmem(keep), in_vmem(received))


def lift_kernel(heads, query_ref, key_up_ref, row_ref, nope_ref, rope_ref):
    tokens, every, width = query_ref.shape
    nope, latent = key_up_ref.shape[1:]
    nope_ref[...] = query_ref[:, :, :nope].astype(F32).reshape(tokens * every, nope)
    rope_ref[:, : width - nope] = (
        query_ref[:, :, nope:].astype(F32).reshape(tokens * every, width - nope)
    )
    for index, head in enumerate(heads):
        at = slice(index * tokens, (index + 1) * tokens)
        part = nope_ref[pl.ds(head, tokens, stride=every), :].astype(BF16)
        row_ref[at, :latent] = dot(part, key_up_ref[head]).astype(BF16)
        rope = rope_ref[pl.ds(head, tokens, stride=every), :]
        row_ref[at, latent:] = rope[:, : width - nope].astype(BF16)


def prompt_lift(heads, prompt_query, key_up):
    tokens, every, width = prompt_query.shape
    nope, latent_width = key_up.shape[1:]
    return pl.pallas_call(
        functools.partial(lift_kernel, heads),
        out_shape=pltpu.VMEM((tokens * len(heads), latent_width + width - nope), BF16),
        in_specs=[VMEM] * 2,
        out_specs=VMEM,
        scratch_shapes=[
            pltpu.VMEM((tokens * every, nope), F32),
            pltpu.VMEM((tokens * every, LANES), F32),
        ],
        compiler_params=params(8),
        cost_estimate=pl.CostEstimate(
            flops=8 * 10**8, bytes_accessed=3 * 10**6, transcendentals=0
        ),
        name="prompt_lift",
    )(in_vmem(prompt_query), in_vmem(key_up))


def attend(
    rate, group, heads, row_refs, key_ref, key_pos_ref, query_pos_ref, value_up_ref, put
):
    tokens = query_pos_ref.shape[0]
    count = key_ref.shape[0]
    latent = value_up_ref.shape[1]
    visible = (key_pos_ref[:1, :] <= query_pos_ref[:, :1])[None]

    def score(first):
        first = first * tokens
        for rows in row_refs:
            if first < rows.shape[0]:
                return dot_nt(rows[first : first + group * tokens, :], key_ref[...])
            first -= rows.shape[0]

    firsts = list(range(heads.start, heads.stop, group))
    ahead = score(firsts[0])
    for first in firsts:
        scores = ahead
        if first != firsts[-1]:
            ahead = score(first + group)
        scores = jnp.where(visible, scores.reshape(group, tokens, count), HIDDEN)
        scores = scores.reshape(group * tokens, count)
        weights = jnp.exp2((scores - jnp.max(scores, axis=1, keepdims=True)) * rate)
        inverse = 1.0 / jnp.sum(weights, axis=1, keepdims=True)
        mixed = dot(weights.astype(BF16), key_ref[:, :latent]).astype(BF16)
        for index in range(group):
            part = slice(index * tokens, (index + 1) * tokens)
            value = dot(mixed[part], value_up_ref[first + index]) * inverse[part]
            put(first + index, value.astype(BF16))


def front_kernel(
    rate,
    group,
    heads,
    early_ref,
    late_ref,
    key_ref,
    key_pos_ref,
    query_pos_ref,
    value_up_ref,
    out_ref,
):
    width = value_up_ref.shape[2]

    def put(head, value):
        at = (head - heads.start) * width
        out_ref[:, at : at + width] = value

    attend(
        rate,
        group,
        heads,
        (early_ref, late_ref),
        key_ref,
        key_pos_ref,
        query_pos_ref,
        value_up_ref,
        put,
    )


def prompt_front(rate, group, heads, rows, keys, key_pos, query_pos, value_up):
    tokens = query_pos.shape[0]
    return pl.pallas_call(
        functools.partial(front_kernel, rate, group, heads),
        out_shape=pltpu.VMEM((tokens, len(heads) * value_up.shape[2]), BF16),
        in_specs=[VMEM] * 6,
        out_specs=VMEM,
        compiler_params=params(16),
        cost_estimate=pl.CostEstimate(
            flops=4 * 10**8, bytes_accessed=3 * 10**6, transcendentals=3 * 10**5
        ),
        name="prompt_front",
    )(*(in_vmem(v) for v in (*rows, keys, key_pos, query_pos, value_up)))


def back_kernel(
    rate,
    group,
    heads,
    early_ref,
    late_ref,
    key_ref,
    key_pos_ref,
    query_pos_ref,
    value_up_ref,
    front_ref,
    keep_ref,
    received_ref,
    out_hbm,
    steps_hbm,
    back_ref,
    steps_ref,
    sems,
):
    width = value_up_ref.shape[2]
    edge = heads.start * width
    copies = []

    def send(source, target):
        copies.append(pltpu.make_async_copy(source, target, sems.at[len(copies)]))
        copies[-1].start()

    send(front_ref, out_hbm.at[:, :edge])
    share = keep_ref[0] + received_ref[0].astype(F32)
    steps, requests, _ = steps_ref.shape
    for step in range(steps):
        rows = [share[at : at + 1] for at in range(step, steps * requests, steps)]
        steps_ref[step] = jnp.concatenate(rows, axis=0).astype(BF16)
    send(steps_ref, steps_hbm)

    def put(head, value):
        at = (head - heads.start) * width
        back_ref[:, at : at + width] = value
        if (head - heads.start + 1) % group == 0:
            start = at + width - group * width
            send(
                back_ref.at[:, start : at + width],
                out_hbm.at[:, edge + start : edge + at + width],
            )

    attend(
        rate,
        group,
        heads,
        (early_ref, late_ref),
        key_ref,
        key_pos_ref,
        query_pos_ref,
        value_up_ref,
        put,
    )
    for copy in copies:
        copy.wait()


def prompt_back(
    rate, group, heads, steps, rows, keys, key_pos, query_pos, value_up, front, keep, received
):
    tokens = query_pos.shape[0]
    width = value_up.shape[2]
    pairs, columns = keep.shape[1:]
    step_shape = (steps, pairs // steps, columns)
    return pl.pallas_call(
        functools.partial(back_kernel, rate, group, heads),
        out_shape=(
            jax.ShapeDtypeStruct((tokens, heads.stop * width), BF16),
            jax.ShapeDtypeStruct(step_shape, BF16),
        ),
        in_specs=[VMEM] * 9,
        out_specs=[ANY] * 2,
        scratch_shapes=[
            pltpu.VMEM((tokens, len(heads) * width), BF16),
            pltpu.VMEM(step_shape, BF16),
            pltpu.SemaphoreType.DMA((2 + len(heads) // group,)),
        ],
        compiler_params=params(16),
        cost_estimate=pl.CostEstimate(
            flops=8 * 10**8, bytes_accessed=6 * 10**6, transcendentals=3 * 10**5
        ),
        name="prompt_back",
    )(
        *(
            in_vmem(v)
            for v in (*rows, keys, key_pos, query_pos, value_up, front, keep, received)
        )
    )


def per_device(
    prompt_query,
    prompt_latent,
    block_order,
    key_up,
    value_up,
    out_weight,
    step_query,
    cache_latent,
    step_latent,
    cache_length,
    block_dest,
):
    heads, width = prompt_query.shape[1:]
    rate = width ** (-0.5) * math.log2(math.e)
    context_size = lax.axis_size("ctx")
    steps = step_query.shape[0]
    head_size = lax.axis_size("head")
    role_size = lax.axis_size("role")

    rounds = doublings(context_size)
    assert role_size == 2 and context_size >= 4
    (
        running,
        key_up,
        value_up,
        latent,
        half,
        prompt_query,
        key_pos,
        query_pos,
    ) = step_part(
        rate,
        block_order,
        cache_length,
        block_dest,
        step_query,
        key_up,
        jnp.swapaxes(cache_latent, 1, 2),
        prompt_latent,
        step_latent,
        value_up,
        prompt_query,
    )
    edge = heads - heads // 4
    early = edge // 2
    early_rows = prompt_lift(range(early), prompt_query, key_up)
    late_rows = prompt_lift(range(early, heads), prompt_query, key_up)
    rows = (early_rows, late_rows)
    for step in rounds:
        far_running = swap(running, "ctx", step)
        if step != rounds[-1]:
            running = merge_parts(rate, heads, running, far_running)
    far = swap(half, "ctx", 2)
    near = swap(move_rows(join_kernel, 2 * half.shape[0], half, far), "ctx", 1)
    mine = move_rows(join_kernel, 3 * half.shape[0], far, near)
    other = swap(mine, "role", 1)
    keys = move_rows(gather_kernel, 4 * latent.shape[0], latent, mine, other)
    for step in rounds[2:]:
        sent = move_rows(half_kernel, keys.shape[0] // 2, keys)
        received = swap(sent, "ctx", step)
        keys = move_rows(
            extend_kernel, 2 * keys.shape[0], keys, received, swap(received, "role", 1)
        )
    front = prompt_front(rate, early, range(edge), rows, keys, key_pos, query_pos, value_up)
    keep, give = finish_steps(
        rate, heads, head_size * role_size, running, far_running, out_weight
    )
    partial = swap(give, "role", 1)
    for step in reversed(doublings(head_size)):
        keep, give = fold_steps(step, keep, partial)
        partial = swap(give, "head", step)
    return prompt_back(
        rate,
        heads - edge,
        range(edge, heads),
        steps,
        rows,
        keys,
        key_pos,
        query_pos,
        value_up,
        front,
        keep,
        partial,
    )


def solution(mesh):
    return jax.shard_map(
        per_device,
        mesh=mesh,
        in_specs=(
            P(("groups", "ctx"), ("head", "role"), None),
            P(("groups", "ctx"), None),
            P("groups"),
            P(("head", "role"), None, None),
            P(("head", "role"), None, None),
            P(("head", "role"), "ctx"),
            P(None, "groups", ("head", "role"), None),
            P("groups", "ctx", None),
            P(None, "groups", None),
            P("groups"),
            P("groups"),
        ),
        out_specs=(
            P(("groups", "ctx"), ("head", "role")),
            P(None, "groups", ("ctx", "head", "role")),
        ),
        check_vma=False,
    )
```

```python
import functools
import math

import jax
import jax.numpy as jnp
from jax import lax
from jax.experimental import pallas as pl
from jax.experimental.pallas import tpu as pltpu
from jax.sharding import PartitionSpec as P


BF16 = jnp.bfloat16
F32 = jnp.float32
LANES = 128
HIDDEN = -1e30
FLOOR = -1e29
TINY = 1e-30
MIB = 1 << 20

VMEM = pl.BlockSpec(memory_space=pltpu.VMEM)
ANY = pl.BlockSpec(memory_space=pl.ANY)
NT = (((1,), (1,)), ((), ()))


def dot(left, right):
    return jnp.dot(left, right, preferred_element_type=F32)


def dot_nt(left, right):
    return lax.dot_general(left, right, NT, preferred_element_type=F32)


def doublings(size):
    steps = []
    step = 1
    while step < size:
        steps.append(step)
        step *= 2
    assert step == size
    return steps


def swap(value, axis, step):
    size = lax.axis_size(axis)
    return lax.ppermute(value, axis, [(i, i ^ step) for i in range(size)])


def in_hbm(value):
    return pltpu.with_memory_space_constraint(value, pltpu.HBM)


def in_vmem(value):
    return pltpu.with_memory_space_constraint(value, pltpu.VMEM)


def params(mib):
    return pltpu.CompilerParams(vmem_limit_bytes=mib * MIB)


def split_three(value):
    high = value.astype(BF16).astype(F32)
    rest = value - high
    middle = rest.astype(BF16).astype(F32)
    return high, middle, (rest - middle).astype(BF16).astype(F32)


def pick_piece(pieces, piece_ids):
    picked = pieces[-1]
    for index in reversed(range(len(pieces) - 1)):
        picked = jnp.where(piece_ids == index, pieces[index], picked)
    return picked


def step_kernel(
    rate,
    order_hbm,
    length_hbm,
    dest_hbm,
    query_hbm,
    key_up_hbm,
    cache_hbm,
    latent_hbm,
    fresh_hbm,
    value_up_hbm,
    prompt_hbm,
    out_ref,
    key_up_ref,
    value_up_ref,
    latent_ref,
    half_ref,
    prompt_ref,
    key_pos_ref,
    query_pos_ref,
    order_ref,
    length_ref,
    dest_ref,
    query_ref,
    cache_ref,
    fresh_ref,
    nope_ref,
    row_ref,
    extra_ref,
    mixed_ref,
    sems,
):
    steps, requests, heads, width = query_ref.shape
    nope, latent = key_up_ref.shape[1:]
    span = cache_ref.shape[2]
    tokens = latent_ref.shape[0]
    pairs = steps * requests
    rows = pairs * heads
    block = steps * heads
    place = lax.axis_index("ctx")

    copies = []

    def fetch(source, target):
        copies.append(pltpu.make_async_copy(source, target, sems.at[len(copies)]))
        copies[-1].start()
        return copies[-1]

    query_copy = fetch(query_hbm, query_ref)
    chunk = heads // 2
    key_up_copies = [
        fetch(key_up_hbm.at[at : at + chunk], key_up_ref.at[at : at + chunk])
        for at in range(0, heads, chunk)
    ]
    latent_copy = fetch(latent_hbm, latent_ref)
    fresh_copy = fetch(fresh_hbm, fresh_ref)
    scalar_copies = [
        fetch(length_hbm, length_ref),
        fetch(dest_hbm, dest_ref),
        fetch(order_hbm, order_ref),
    ]
    cache_copy = fetch(cache_hbm, cache_ref)
    value_up_copy = fetch(value_up_hbm, value_up_ref)

    query_copy.wait()
    query = query_ref[...].astype(F32)
    query = jnp.concatenate(
        [query[:, request].reshape(block, width) for request in range(requests)], axis=0
    )
    nope_ref[...] = query[:, :nope]
    rope = query[:, nope:]
    for head in range(heads):
        if head % chunk == 0:
            key_up_copies[head // chunk].wait()
        part = nope_ref[pl.ds(head, pairs, stride=heads), :].astype(BF16)
        lifted = dot(part, key_up_ref[head]).astype(BF16).astype(F32)
        for lane in range(0, latent, LANES):
            row_ref[lane // LANES, pl.ds(head, pairs, stride=heads), :] = lifted[
                :, lane : lane + LANES
            ]
    prompt_copy = fetch(prompt_hbm, prompt_ref)
    row_parts = [row_ref[index] for index in range(latent // LANES)] + [rope]
    query_rows = jnp.concatenate(row_parts, axis=1).astype(BF16)

    latent_copy.wait()
    fresh_copy.wait()
    half = half_ref.shape[0]
    for index in range(2):

        @pl.when(lax.axis_index("role") == index)
        def _():
            half_ref[...] = latent_ref[index * half : (index + 1) * half, :]

    extra_ref[:tokens, :] = latent_ref[...].astype(F32)
    for step in range(steps):
        extra_ref[tokens + step * requests : tokens + (step + 1) * requests, :] = fresh_ref[
            step
        ].astype(F32)
    extra = extra_ref[...].astype(BF16)
    more = dot_nt(query_rows, extra)
    for copy in scalar_copies:
        copy.wait()
    column = lax.broadcasted_iota(jnp.int32, more.shape, 1)
    row = lax.broadcasted_iota(jnp.int32, more.shape, 0)
    fresh_id = column - tokens
    seen = ((column < tokens) & (row // block == dest_ref[place])) | (
        (column >= tokens)
        & (fresh_id % requests == row // block)
        & (fresh_id // requests <= row // heads % steps)
        & (place == 0)
    )
    more = jnp.where(seen, more, HIDDEN)
    position = place * span + lax.broadcasted_iota(jnp.int32, (1, span), 1)
    cache_copy.wait()
    scores = [
        jnp.where(
            position < length_ref[request],
            dot(query_rows[request * block : (request + 1) * block], cache_ref[request]),
            HIDDEN,
        )
        for request in range(requests)
    ]
    scores = jnp.concatenate(scores, axis=0)
    high = jnp.maximum(
        jnp.max(scores, axis=1, keepdims=True), jnp.max(more, axis=1, keepdims=True)
    )
    high = jnp.maximum(high, FLOOR)
    weights = jnp.exp2((scores - high) * rate)
    more = jnp.exp2((more - high) * rate)
    total = jnp.sum(weights, axis=1, keepdims=True) + jnp.sum(more, axis=1, keepdims=True)
    weights = weights.astype(BF16)
    mixed = jnp.concatenate(
        [
            dot_nt(weights[request * block : (request + 1) * block], cache_ref[request, :latent])
            for request in range(requests)
        ],
        axis=0,
    )
    mixed = mixed + dot(more.astype(BF16), extra[:, :latent])
    mixed = mixed * (1.0 / jnp.maximum(total, TINY))
    for lane in range(0, latent, LANES):
        mixed_ref[lane // LANES] = mixed[:, lane : lane + LANES]
    high = jnp.broadcast_to(high, (rows, LANES))
    total = jnp.broadcast_to(total, (rows, LANES))

    value_up_copy.wait()
    value_width = value_up_ref.shape[2]
    for head in range(heads):
        parts = [
            mixed_ref[index, pl.ds(head, pairs, stride=heads), :]
            for index in range(latent // LANES)
        ]
        part = jnp.concatenate(parts, axis=1).astype(BF16)
        out_ref[:, head * value_width : (head + 1) * value_width] = dot(
            part, value_up_ref[head]
        ).astype(BF16)
    lane = lax.broadcasted_iota(jnp.int32, (rows, LANES), 1)
    head_of_row = lax.broadcasted_iota(jnp.int32, (rows, LANES), 0) % heads
    pieces = split_three(high) + split_three(total)
    packed = pick_piece(pieces, lane // heads)
    packed = jnp.where((lane % heads == head_of_row) & (lane < 6 * heads), packed, 0.0)
    packed = jnp.sum(packed.reshape(pairs, heads, LANES), axis=1)
    out_ref[:, heads * value_width :] = packed.astype(BF16)

    key_id = lax.broadcasted_iota(jnp.int32, key_pos_ref.shape, 1)
    base = key_id
    for slot in range(key_pos_ref.shape[1] // tokens):
        move = (order_ref[place ^ slot] - slot) * tokens
        base = base + jnp.where(key_id // tokens == slot, move, 0)
    key_pos_ref[...] = base
    query_pos_ref[...] = order_ref[place] * tokens + lax.broadcasted_iota(
        jnp.int32, query_pos_ref.shape, 0
    )
    prompt_copy.wait()


def step_part(
    rate,
    block_order,
    cache_length,
    block_dest,
    step_query,
    key_up,
    cache,
    latent,
    fresh,
    value_up,
    prompt_query,
):
    steps, requests, heads, _ = step_query.shape
    nope, latent_width = key_up.shape[1:]
    full = cache.shape[1]
    tokens = latent.shape[0]
    pairs = steps * requests
    rows = pairs * heads
    shape = pltpu.VMEM
    return pl.pallas_call(
        functools.partial(step_kernel, rate),
        out_shape=(
            shape((pairs, heads * value_up.shape[2] + LANES), BF16),
            shape(key_up.shape, BF16),
            shape(value_up.shape, BF16),
            shape(latent.shape, BF16),
            shape((tokens // 2, full), BF16),
            shape(prompt_query.shape, BF16),
            shape((8, tokens * lax.axis_size("ctx")), jnp.int32),
            shape((tokens, LANES), jnp.int32),
        ),
        in_specs=[ANY] * 10,
        out_specs=[VMEM] * 8,
        scratch_shapes=[
            pltpu.SMEM(block_order.shape, jnp.int32),
            pltpu.SMEM(cache_length.shape, jnp.int32),
            pltpu.SMEM(block_dest.shape, jnp.int32),
            pltpu.VMEM(step_query.shape, BF16),
            pltpu.VMEM(cache.shape, BF16),
            pltpu.VMEM(fresh.shape, BF16),
            pltpu.VMEM((rows, nope), F32),
            pltpu.VMEM((latent_width // LANES, rows, LANES), F32),
            pltpu.VMEM((tokens + pairs, full), F32),
            pltpu.VMEM((latent_width // LANES, rows, LANES), F32),
            pltpu.SemaphoreType.DMA((11,)),
        ],
        compiler_params=params(16),
        cost_estimate=pl.CostEstimate(flops=10**9, bytes_accessed=10**7, transcendentals=10**5),
        name="step_part",
    )(
        *(
            in_hbm(value)
            for value in (
                block_order,
                cache_length,
                block_dest,
                step_query,
                key_up,
                cache,
                latent,
                fresh,
                value_up,
                prompt_query,
            )
        )
    )


def read_stats(packed, heads):
    def piece(index):
        if index == 0:
            return packed
        return pltpu.roll(packed, LANES - index * heads, 1)

    return piece(0) + piece(1) + piece(2), piece(3) + piece(4) + piece(5)


def merge(rate, first_ref, second_ref, heads):
    split = first_ref.shape[1] - LANES
    value_width = split // heads
    high_a, total_a = read_stats(first_ref[:, split:].astype(F32), heads)
    high_b, total_b = read_stats(second_ref[:, split:].astype(F32), heads)
    high = jnp.maximum(high_a, high_b)
    share_a = total_a * jnp.exp2((high_a - high) * rate)
    share_b = total_b * jnp.exp2((high_b - high) * rate)
    total = share_a + share_b
    inverse = 1.0 / jnp.maximum(total, TINY)
    share_a = share_a * inverse
    share_b = share_b * inverse
    merged = []
    for head in range(heads):
        at = slice(head * value_width, (head + 1) * value_width)
        merged.append(
            (
                first_ref[:, at].astype(F32) * share_a[:, head : head + 1]
                + second_ref[:, at].astype(F32) * share_b[:, head : head + 1]
            ).astype(BF16)
        )
    return merged, high, total


def merge_kernel(rate, heads, first_ref, second_ref, out_ref):
    merged, high, total = merge(rate, first_ref, second_ref, heads)
    value_width = merged[0].shape[1]
    for head in range(heads):
        out_ref[:, head * value_width : (head + 1) * value_width] = merged[head]
    pieces = split_three(high) + split_three(total)
    lane = lax.broadcasted_iota(jnp.int32, high.shape, 1)
    moved = [p if i == 0 else pltpu.roll(p, i * heads, 1) for i, p in enumerate(pieces)]
    packed = jnp.where(lane < 6 * heads, pick_piece(moved, lane // heads), 0.0)
    out_ref[:, heads * value_width :] = packed.astype(BF16)


def merge_parts(rate, heads, first, second):
    return pl.pallas_call(
        functools.partial(merge_kernel, rate, heads),
        out_shape=pltpu.VMEM(first.shape, BF16),
        in_specs=[VMEM] * 2,
        out_specs=VMEM,
        compiler_params=params(2),
        cost_estimate=pl.CostEstimate(
            flops=8 * 10**9, bytes_accessed=2 * 10**5, transcendentals=10**4
        ),
        name="merge_parts",
    )(in_vmem(first), in_vmem(second))


def join_kernel(first_ref, second_ref, out_ref):
    rows = first_ref.shape[0]
    out_ref[:rows, :] = first_ref[...]
    out_ref[rows:, :] = second_ref[...]


def gather_kernel(own_ref, mine_ref, other_ref, out_ref):
    tokens = own_ref.shape[0]
    half = tokens // 2
    out_ref[:tokens, :] = own_ref[...]
    for index, sources in enumerate(((mine_ref, other_ref), (other_ref, mine_ref))):

        @pl.when(lax.axis_index("role") == index)
        def _():
            for part, source in enumerate(sources):
                for place, slot in enumerate((2, 1, 3)):
                    at = slot * tokens + part * half
                    out_ref[at : at + half, :] = source[place * half : (place + 1) * half, :]


def half_kernel(keys_ref, out_ref):
    rows = out_ref.shape[0]
    for index in range(2):

        @pl.when(lax.axis_index("role") == index)
        def _():
            out_ref[...] = keys_ref[index * rows : (index + 1) * rows, :]


def extend_kernel(keys_ref, mine_ref, other_ref, out_ref):
    rows = keys_ref.shape[0]
    half = mine_ref.shape[0]
    out_ref[:rows, :] = keys_ref[...]
    for index, sources in enumerate(((mine_ref, other_ref), (other_ref, mine_ref))):

        @pl.when(lax.axis_index("role") == index)
        def _():
            out_ref[rows : rows + half, :] = sources[0][...]
            out_ref[rows + half :, :] = sources[1][...]


def move_rows(body, rows, *sources):
    return pl.pallas_call(
        body,
        out_shape=pltpu.VMEM((rows, sources[0].shape[1]), BF16),
        in_specs=[VMEM] * len(sources),
        out_specs=VMEM,
        compiler_params=params(1),
        cost_estimate=pl.CostEstimate(flops=10**4, bytes_accessed=4 * 10**5, transcendentals=0),
    )(*(in_vmem(source) for source in sources))


def finish_kernel(
    rate, heads, parts, first_ref, second_ref, weight_ref, keep_ref, give_ref
):
    merged, _, _ = merge(rate, first_ref, second_ref, heads)
    rows = jnp.concatenate(merged, axis=1)
    product = dot(rows, weight_ref[...])
    width = product.shape[1] // parts
    upper = lax.axis_index("role") == 1
    for index in range(parts // 2):
        low, high = (
            product[:, part * width : (part + 1) * width] for part in (2 * index, 2 * index + 1)
        )
        keep_ref[index] = jnp.where(upper, high, low)
        give_ref[index] = jnp.where(upper, low, high).astype(BF16)


def finish_steps(rate, heads, parts, first, second, weight):
    pairs = first.shape[0]
    shape = (parts // 2, pairs, weight.shape[1] // parts)
    return pl.pallas_call(
        functools.partial(finish_kernel, rate, heads, parts),
        out_shape=(pltpu.VMEM(shape, F32), pltpu.VMEM(shape, BF16)),
        in_specs=[VMEM] * 3,
        out_specs=[VMEM] * 2,
        compiler_params=params(4),
        cost_estimate=pl.CostEstimate(
            flops=5 * 10**8, bytes_accessed=8 * 10**6, transcendentals=10**4
        ),
        name="finish_steps",
    )(*(in_vmem(v) for v in (first, second, weight)))


def fold_kernel(step, keep_ref, received_ref, new_keep_ref, give_ref):
    share = keep_ref[...] + received_ref[...].astype(F32)
    middle = share.shape[0] // 2
    upper = lax.axis_index("head") & step != 0
    new_keep_ref[...] = jnp.where(upper, share[middle:], share[:middle])
    give_ref[...] = jnp.where(upper, share[:middle], share[middle:]).astype(BF16)


def fold_steps(step, keep, received):
    shape = (keep.shape[0] // 2, *keep.shape[1:])
    return pl.pallas_call(
        functools.partial(fold_kernel, step),
        out_shape=(pltpu.VMEM(shape, F32), pltpu.VMEM(shape, BF16)),
        in_specs=[VMEM] * 2,
        out_specs=[VMEM] * 2,
        compiler_params=params(1),
        cost_estimate=pl.CostEstimate(flops=10**5, bytes_accessed=10**5, transcendentals=0),
        name="fold_steps",
    )(in_vmem(keep), in_vmem(received))


def lift_kernel(heads, query_ref, key_up_ref, row_ref, nope_ref, rope_ref):
    tokens, every, width = query_ref.shape
    nope, latent = key_up_ref.shape[1:]
    nope_ref[...] = query_ref[:, :, :nope].astype(F32).reshape(tokens * every, nope)
    rope_ref[:, : width - nope] = (
        query_ref[:, :, nope:].astype(F32).reshape(tokens * every, width - nope)
    )
    for index, head in enumerate(heads):
        at = slice(index * tokens, (index + 1) * tokens)
        part = nope_ref[pl.ds(head, tokens, stride=every), :].astype(BF16)
        row_ref[at, :latent] = dot(part, key_up_ref[head]).astype(BF16)
        rope = rope_ref[pl.ds(head, tokens, stride=every), :]
        row_ref[at, latent:] = rope[:, : width - nope].astype(BF16)


def prompt_lift(heads, prompt_query, key_up):
    tokens, every, width = prompt_query.shape
    nope, latent_width = key_up.shape[1:]
    return pl.pallas_call(
        functools.partial(lift_kernel, heads),
        out_shape=pltpu.VMEM((tokens * len(heads), latent_width + width - nope), BF16),
        in_specs=[VMEM] * 2,
        out_specs=VMEM,
        scratch_shapes=[
            pltpu.VMEM((tokens * every, nope), F32),
            pltpu.VMEM((tokens * every, LANES), F32),
        ],
        compiler_params=params(8),
        cost_estimate=pl.CostEstimate(
            flops=8 * 10**8, bytes_accessed=3 * 10**6, transcendentals=0
        ),
        name="prompt_lift",
    )(in_vmem(prompt_query), in_vmem(key_up))


def attend(
    rate, group, heads, row_refs, key_ref, key_pos_ref, query_pos_ref, value_up_ref, put
):
    tokens = query_pos_ref.shape[0]
    count = key_ref.shape[0]
    latent = value_up_ref.shape[1]
    visible = (key_pos_ref[:1, :] <= query_pos_ref[:, :1])[None]

    def score(first):
        first = first * tokens
        for rows in row_refs:
            if first < rows.shape[0]:
                return dot_nt(rows[first : first + group * tokens, :], key_ref[...])
            first -= rows.shape[0]

    firsts = list(range(heads.start, heads.stop, group))
    ahead = score(firsts[0])
    for first in firsts:
        scores = ahead
        if first != firsts[-1]:
            ahead = score(first + group)
        scores = jnp.where(visible, scores.reshape(group, tokens, count), HIDDEN)
        scores = scores.reshape(group * tokens, count)
        weights = jnp.exp2((scores - jnp.max(scores, axis=1, keepdims=True)) * rate)
        inverse = 1.0 / jnp.sum(weights, axis=1, keepdims=True)
        mixed = dot(weights.astype(BF16), key_ref[:, :latent]).astype(BF16)
        for index in range(group):
            part = slice(index * tokens, (index + 1) * tokens)
            value = dot(mixed[part], value_up_ref[first + index]) * inverse[part]
            put(first + index, value.astype(BF16))


def front_kernel(
    rate,
    group,
    heads,
    early_ref,
    late_ref,
    key_ref,
    key_pos_ref,
    query_pos_ref,
    value_up_ref,
    out_ref,
):
    width = value_up_ref.shape[2]

    def put(head, value):
        at = (head - heads.start) * width
        out_ref[:, at : at + width] = value

    attend(
        rate,
        group,
        heads,
        (early_ref, late_ref),
        key_ref,
        key_pos_ref,
        query_pos_ref,
        value_up_ref,
        put,
    )


def prompt_front(rate, group, heads, rows, keys, key_pos, query_pos, value_up):
    tokens = query_pos.shape[0]
    return pl.pallas_call(
        functools.partial(front_kernel, rate, group, heads),
        out_shape=pltpu.VMEM((tokens, len(heads) * value_up.shape[2]), BF16),
        in_specs=[VMEM] * 6,
        out_specs=VMEM,
        compiler_params=params(16),
        cost_estimate=pl.CostEstimate(
            flops=4 * 10**8, bytes_accessed=3 * 10**6, transcendentals=3 * 10**5
        ),
        name="prompt_front",
    )(*(in_vmem(v) for v in (*rows, keys, key_pos, query_pos, value_up)))


def back_kernel(
    rate,
    group,
    heads,
    early_ref,
    late_ref,
    key_ref,
    key_pos_ref,
    query_pos_ref,
    value_up_ref,
    front_ref,
    keep_ref,
    received_ref,
    out_hbm,
    steps_hbm,
    back_ref,
    steps_ref,
    sems,
):
    width = value_up_ref.shape[2]
    edge = heads.start * width
    copies = []

    def send(source, target):
        copies.append(pltpu.make_async_copy(source, target, sems.at[len(copies)]))
        copies[-1].start()

    send(front_ref, out_hbm.at[:, :edge])
    share = keep_ref[0] + received_ref[0].astype(F32)
    steps, requests, _ = steps_ref.shape
    for step in range(steps):
        rows = [share[at : at + 1] for at in range(step, steps * requests, steps)]
        steps_ref[step] = jnp.concatenate(rows, axis=0).astype(BF16)
    send(steps_ref, steps_hbm)

    def put(head, value):
        at = (head - heads.start) * width
        back_ref[:, at : at + width] = value
        if (head - heads.start + 1) % group == 0:
            start = at + width - group * width
            send(
                back_ref.at[:, start : at + width],
                out_hbm.at[:, edge + start : edge + at + width],
            )

    attend(
        rate,
        group,
        heads,
        (early_ref, late_ref),
        key_ref,
        key_pos_ref,
        query_pos_ref,
        value_up_ref,
        put,
    )
    for copy in copies:
        copy.wait()


def prompt_back(
    rate, group, heads, steps, rows, keys, key_pos, query_pos, value_up, front, keep, received
):
    tokens = query_pos.shape[0]
    width = value_up.shape[2]
    pairs, columns = keep.shape[1:]
    step_shape = (steps, pairs // steps, columns)
    return pl.pallas_call(
        functools.partial(back_kernel, rate, group, heads),
        out_shape=(
            jax.ShapeDtypeStruct((tokens, heads.stop * width), BF16),
            jax.ShapeDtypeStruct(step_shape, BF16),
        ),
        in_specs=[VMEM] * 9,
        out_specs=[ANY] * 2,
        scratch_shapes=[
            pltpu.VMEM((tokens, len(heads) * width), BF16),
            pltpu.VMEM(step_shape, BF16),
            pltpu.SemaphoreType.DMA((2 + len(heads) // group,)),
        ],
        compiler_params=params(16),
        cost_estimate=pl.CostEstimate(
            flops=8 * 10**8, bytes_accessed=6 * 10**6, transcendentals=3 * 10**5
        ),
        name="prompt_back",
    )(
        *(
            in_vmem(v)
            for v in (*rows, keys, key_pos, query_pos, value_up, front, keep, received)
        )
    )


def per_device(
    prompt_query,
    prompt_latent,
    block_order,
    key_up,
    value_up,
    out_weight,
    step_query,
    cache_latent,
    step_latent,
    cache_length,
    block_dest,
):
    heads, width = prompt_query.shape[1:]
    rate = width ** (-0.5) * math.log2(math.e)
    context_size = lax.axis_size("ctx")
    steps = step_query.shape[0]
    head_size = lax.axis_size("head")
    role_size = lax.axis_size("role")

    rounds = doublings(context_size)
    assert role_size == 2 and context_size >= 4
    (
        running,
        key_up,
        value_up,
        latent,
        half,
        prompt_query,
        key_pos,
        query_pos,
    ) = step_part(
        rate,
        block_order,
        cache_length,
        block_dest,
        step_query,
        key_up,
        jnp.swapaxes(cache_latent, 1, 2),
        prompt_latent,
        step_latent,
        value_up,
        prompt_query,
    )
    group = 4 if heads % 16 == 0 else 2 if heads % 8 == 0 else 1
    edge = heads - heads // 4
    early = heads // 2
    early_rows = prompt_lift(range(early), prompt_query, key_up)
    late_rows = prompt_lift(range(early, heads), prompt_query, key_up)
    rows = (early_rows, late_rows)
    for step in rounds:
        far_running = swap(running, "ctx", step)
        if step != rounds[-1]:
            running = merge_parts(rate, heads, running, far_running)
    far = swap(half, "ctx", 2)
    near = swap(move_rows(join_kernel, 2 * half.shape[0], half, far), "ctx", 1)
    mine = move_rows(join_kernel, 3 * half.shape[0], far, near)
    other = swap(mine, "role", 1)
    keys = move_rows(gather_kernel, 4 * latent.shape[0], latent, mine, other)
    for step in rounds[2:]:
        sent = move_rows(half_kernel, keys.shape[0] // 2, keys)
        received = swap(sent, "ctx", step)
        keys = move_rows(
            extend_kernel, 2 * keys.shape[0], keys, received, swap(received, "role", 1)
        )
    front = prompt_front(rate, group, range(edge), rows, keys, key_pos, query_pos, value_up)
    keep, give = finish_steps(
        rate, heads, head_size * role_size, running, far_running, out_weight
    )
    partial = swap(give, "role", 1)
    for step in reversed(doublings(head_size)):
        keep, give = fold_steps(step, keep, partial)
        partial = swap(give, "head", step)
    return prompt_back(
        rate,
        group,
        range(edge, heads),
        steps,
        rows,
        keys,
        key_pos,
        query_pos,
        value_up,
        front,
        keep,
        partial,
    )


def solution(mesh):
    return jax.shard_map(
        per_device,
        mesh=mesh,
        in_specs=(
            P(("groups", "ctx"), ("head", "role"), None),
            P(("groups", "ctx"), None),
            P("groups"),
            P(("head", "role"), None, None),
            P(("head", "role"), None, None),
            P(("head", "role"), "ctx"),
            P(None, "groups", ("head", "role"), None),
            P("groups", "ctx", None),
            P(None, "groups", None),
            P("groups"),
            P("groups"),
        ),
        out_specs=(
            P(("groups", "ctx"), ("head", "role")),
            P(None, "groups", ("ctx", "head", "role")),
        ),
        check_vma=False,
    )
```
